32 devices in a mesh: lat: 4 (over y, x), lon: 8 (over z, core).
Axes of the slice: x: 2, y: 2, z: 4, core: 2. Of those that a mesh axis runs over, the one named last changes fastest.
Arguments:
- right_side: float32 [512, 2048], P('lat', 'lon'), may hold values from -12 to 12
- diagonal: float32 [512, 2048], P('lat', 'lon'), may hold values from 0.2 to 2
- east_coef: float32 [512, 2048], P('lat', 'lon'), may hold values from 0.5 to 2
- north_coef: float32 [512, 2048], P('lat', 'lon'), may hold values from 0.5 to 2
- land_sea: int32 [512, 2048], P('lat', 'lon'), may hold values 0 or 1
- fold_partner: int32 [2048], P('lon'), may hold values from 0 to 2047, as said below
Outputs:
- solution_field: float32 [512, 2048], P('lat', 'lon')
- residual: float32 [512, 2048], P('lat', 'lon')
The draws below stay inside these ranges and needn't reach their ends.
Inputs may be any that keep to these rules, and one draw needn't show every extreme that they name: fold_partner[fold_partner[i]] = i and fold_partner[i] != i for every column i, and fold_partner[i] // 256 = 7 - i // 256.
All inputs are finite; a program needn't handle non-finite values. No bound on the sum of `land_sea` on one device may be relied on, other than what follows from the above.
Results may differ from the reference program's by a relative error of at most 0.00019.
Values sent between devices are 32-bit elements; how exact they have to be, the bound alone decides.
A program may use at most 64 MiB of HBM per device.

```python
import math
import jax
import jax.numpy as jnp

CI = 256
ITERS = 4
NJ = 512
NI = 2048


def draw_right_side(key, part):
    first_key, second_key, third_key = jax.random.split(key, 3)
    row_pos = jnp.arange(NJ, dtype=jnp.float32) / NJ
    col_pos = jnp.arange(NI, dtype=jnp.float32) / NI
    row_scale = jnp.exp(0.6 * row_pos - 0.6 + jax.random.uniform(first_key, (NJ,), jnp.float32, -0.6, 0.6))
    col_scale = jnp.exp(0.6 * col_pos - 0.6 + jax.random.uniform(second_key, (NI,), jnp.float32, -0.6, 0.6))
    scaled = row_scale[:, None] * col_scale[None, :]
    values = jax.random.normal(third_key, (NJ, NI), jnp.float32) * scaled
    return jnp.clip(values, -12.0, 12.0)


def draw_fold_partner(key, part):
    block_count = NI // CI
    pair_count = block_count // 2
    pair_keys = jax.random.split(key, pair_count)

    def mirror_order(subkey):
        return jax.random.permutation(subkey, CI)
    shuffled = jax.vmap(mirror_order)(pair_keys).astype(jnp.int32)
    pair_ids = jnp.arange(pair_count, dtype=jnp.int32)
    lower_cols = (pair_ids[:, None] * CI + jnp.arange(CI, dtype=jnp.int32)[None, :]).reshape(-1)
    upper_cols = ((block_count - 1 - pair_ids)[:, None] * CI + shuffled).reshape(-1)
    partner = jnp.zeros((NI,), jnp.int32).at[lower_cols].set(upper_cols)
    return partner.at[upper_cols].set(lower_cols)


def plant(array, own_key, least, top_value):
    longest = array.shape.index(max(array.shape))
    spots = []
    for shift in (0, 1):
        where = [jax.random.randint(jax.random.fold_in(own_key, axis), (), 0, length) for axis, length in enumerate(array.shape)]
        where[longest] = (where[longest] + shift) % array.shape[longest]
        spots.append(tuple(where))
    return array.at[spots[0]].set(least).at[spots[1]].set(top_value)


def levels(key, shape, cuts, least, largest):
    loudness, own = 1.0, jax.random.fold_in(key, 6)
    for axis_at, parts in cuts:
        heights = jnp.exp(jax.random.uniform(jax.random.fold_in(own, axis_at), (parts,), jnp.float32, least / len(cuts), largest / len(cuts)))
        loudness = loudness * jnp.repeat(heights, shape[axis_at] // parts).reshape([-1 if axis == axis_at else 1 for axis in range(len(shape))])
    return loudness


def setup_inputs(seed: int = 0) -> dict:
    key_of = jax.random.split(jax.random.key(seed), 7)
    right_side = draw_right_side(jax.random.fold_in(key_of[6], 71), 0)
    diagonal = jnp.clip(jnp.exp(math.log(2.0) - 2.3025851 * jax.random.uniform(key_of[1], (NJ, NI), jnp.float32) ** levels(key_of[1], (NJ, NI), ((0, 4), (1, 8)), -0.2, 0.2)), 0.2, 2.0)
    east_coef = jnp.clip(jnp.exp(math.log(2.0) - 1.3862944 * jax.random.uniform(key_of[2], (NJ, NI), jnp.float32) ** levels(key_of[2], (NJ, NI), ((0, 4), (1, 8)), -0.2, 0.2)), 0.5, 2.0)
    north_coef = jnp.clip(jnp.exp(math.log(2.0) - 1.3862944 * jax.random.uniform(key_of[3], (NJ, NI), jnp.float32) ** levels(key_of[3], (NJ, NI), ((0, 4), (1, 8)), -0.2, 0.2)), 0.5, 2.0)
    land_sea = plant((jax.random.randint(key_of[4], (NJ, NI), 0, 10) < 7).astype(jnp.int32), jax.random.fold_in(key_of[4], 1), 0, 1)
    fold_partner = draw_fold_partner(jax.random.fold_in(key_of[6], 71), 0)
    return {"right_side": right_side, "diagonal": diagonal, "east_coef": east_coef, "north_coef": north_coef, "land_sea": land_sea, "fold_partner": fold_partner}


def spread_of(masked, east_coef, north_coef, fold_partner):
    west_coef = jnp.roll(east_coef, 1, axis=1)
    north_inner = north_coef.at[-1].set(0.0)
    blank = jnp.zeros_like(masked[:1])
    north_vals = jnp.concatenate([masked[1:], blank], axis=0)
    south_vals = jnp.concatenate([blank, masked[:-1]], axis=0)
    south_coef = jnp.concatenate([jnp.zeros_like(north_inner[:1]), north_inner[:-1]], axis=0)
    top_coef = north_coef[-1]
    fold_coef = 0.5 * (top_coef + top_coef[fold_partner])
    spread = east_coef * (masked - jnp.roll(masked, -1, axis=1)) + west_coef * (masked - jnp.roll(masked, 1, axis=1))
    spread = spread + north_inner * (masked - north_vals) + south_coef * (masked - south_vals)
    last_row = masked[-1]
    return spread.at[-1].add(fold_coef * (last_row - last_row[fold_partner]))


def reference(right_side, diagonal, east_coef, north_coef, land_sea, fold_partner):
    ocean = land_sea.astype(jnp.float32)

    def operate(surface):
        masked = ocean * surface
        return diagonal * surface + ocean * spread_of(masked, east_coef, north_coef, fold_partner)

    solution_field = jnp.zeros_like(right_side)
    residual = right_side
    direction = right_side
    norm_now = jnp.sum(residual * residual)
    for iteration in range(ITERS):
        image = operate(direction)
        alpha = norm_now / jnp.sum(direction * image)
        solution_field = solution_field + alpha * direction
        residual = residual - alpha * image
        norm_next = jnp.sum(residual * residual)
        direction = residual + (norm_next / norm_now) * direction
        norm_now = norm_next
    return solution_field, residual
```

```python
import jax
import jax.numpy as jnp
from jax import lax
from jax.experimental import pallas as pl
from jax.experimental.pallas import tpu as pltpu
from jax.sharding import PartitionSpec as P

ITERS = 4
MESH = pl.DeviceIdType.MESH
NORTH, SOUTH, EAST, WEST = range(4)
f32 = jnp.float32


def kernel(lats, lons, rhs_hbm, diag_hbm, east_hbm, north_hbm, land_hbm, partner_hbm,
           sol_ref, res_ref,
           rhs, diag, east, north, land, partner, load_sem,
           held, cols_out, rows_in, cols_in, coef_cols, coef_rows, coef_cols_in,
           send_sem, recv_sem, coef_send, coef_recv,
           part_out, part_in, part_send, part_recv):
    rows, cols = rhs.shape
    count = lats * lons
    lat, lon = lax.axis_index("lat"), lax.axis_index("lon")
    me = lat * lons + lon
    on_top, on_bottom = lat == lats - 1, lat == 0

    loads = [
        pltpu.make_async_copy(src, dst, load_sem.at[i])
        for i, (src, dst) in enumerate(
            ((rhs_hbm, rhs), (land_hbm, land), (east_hbm, east), (north_hbm, north),
             (partner_hbm, partner), (diag_hbm, diag)))
    ]
    for load in loads:
        load.start()

    barrier = pltpu.get_barrier_semaphore()

    def device(shift):
        other = lax.rem(me + shift, count)
        return (other // lons, lax.rem(other, lons))

    def greet(shift, carry):
        pl.semaphore_signal(barrier, inc=1, device_id=device(shift), device_id_type=MESH)
        return carry

    lax.fori_loop(1, count, greet, 0)

    east_id = (lat, lax.rem(lon + 1, lons))
    west_id = (lat, lax.rem(lon + lons - 1, lons))
    north_id = (lax.rem(lat + 1, lats), lon)
    south_id = (lax.rem(lat + lats - 1, lats), lon)
    fold_id = (lat, lons - 1 - lon)

    row_ids = lax.broadcasted_iota(jnp.int32, (rows, cols), 0)
    col_ids = lax.broadcasted_iota(jnp.int32, (rows, cols), 1)
    eye = lax.broadcasted_iota(jnp.int32, (rows, rows), 0) == lax.broadcasted_iota(
        jnp.int32, (rows, rows), 1)
    lane = lax.broadcasted_iota(jnp.int32, (1, 128), 1)

    def flat(column):
        return jnp.sum(jnp.where(eye, column, 0.0), axis=0, keepdims=True)

    def upright(row):
        return jnp.sum(jnp.where(eye, row, 0.0), axis=1, keepdims=True)

    for load in loads:
        load.wait()
    ocean = land[...].astype(f32)
    east_c = east[...]
    coef_cols[...] = jnp.broadcast_to(flat(east_c[:, cols - 1:]), (8, rows))
    held[0] = ocean * rhs[...]

    own = lax.rem(partner[...], cols)
    lower = jnp.broadcast_to(lax.rem(own, 128), (8, cols))
    panel = jnp.broadcast_to(own // 128, (8, cols))

    def mirrored(block):
        pieces = []
        for at in range(0, cols, 128):
            index = lower[:, at:at + 128]
            which = panel[:, at:at + 128]
            picked = jnp.zeros((8, 128), f32)
            for k in range(cols // 128):
                found = jnp.take_along_axis(block[:, k * 128:(k + 1) * 128], index, axis=1)
                picked = jnp.where(which == k, found, picked)
            pieces.append(picked)
        return jnp.concatenate(pieces, axis=1)[7:8]

    @pl.when(on_bottom)
    def _():
        for k in range(ITERS):
            rows_in[k, SOUTH] = jnp.zeros((8, cols), f32)
        coef_rows[1] = jnp.zeros((8, cols), f32)

    pl.semaphore_wait(barrier, count - 1)

    def remote(src, dst, send, recv, to):
        return pltpu.make_async_remote_copy(
            src_ref=src, dst_ref=dst, send_sem=send, recv_sem=recv,
            device_id=to, device_id_type=MESH)

    def halo_copies(k):
        top, base = held.at[k, pl.ds(rows - 8, 8)], held.at[k, pl.ds(0, 8)]
        sems = lambda way: (send_sem.at[k, way], recv_sem.at[k, way])
        to_east = remote(cols_out.at[k, 0], cols_in.at[k, 0], *sems(WEST), east_id)
        to_west = remote(cols_out.at[k, 1], cols_in.at[k, 1], *sems(EAST), west_id)
        to_fold = remote(top, rows_in.at[k, NORTH], *sems(NORTH), fold_id)
        to_north = remote(top, rows_in.at[k, SOUTH], send_sem.at[k, NORTH], recv_sem.at[k, SOUTH], north_id)
        to_south = remote(base, rows_in.at[k, NORTH], send_sem.at[k, SOUTH], recv_sem.at[k, NORTH], south_id)
        return to_east, to_west, to_fold, to_north, to_south

    coef_east = remote(coef_cols, coef_cols_in, coef_send.at[0], coef_recv.at[0], east_id)
    coef_top = north.at[pl.ds(rows - 8, 8)]
    coef_fold = remote(coef_top, coef_rows.at[0], coef_send.at[1], coef_recv.at[1], fold_id)
    coef_north = remote(coef_top, coef_rows.at[1], coef_send.at[1], coef_recv.at[2], north_id)

    coef_east.start()

    @pl.when(on_top)
    def _():
        coef_fold.start()

    @pl.when(jnp.logical_not(on_top))
    def _():
        coef_north.start()

    def send_halo(k):
        to_east, to_west, to_fold, to_north, to_south = halo_copies(k)

        @pl.when(on_top)
        def _():
            to_fold.start()

        @pl.when(jnp.logical_not(on_top))
        def _():
            to_north.start()

        @pl.when(jnp.logical_not(on_bottom))
        def _():
            to_south.start()

        masked = held[k]
        cols_out[k, 0] = jnp.broadcast_to(flat(masked[:, cols - 1:]), (8, rows))
        cols_out[k, 1] = jnp.broadcast_to(flat(masked[:, :1]), (8, rows))
        to_east.start()
        to_west.start()

    def take_halo(k):
        to_east, to_west, to_fold, to_north, to_south = halo_copies(k)
        to_east.wait_recv()
        to_west.wait_recv()
        to_south.wait_recv()

        @pl.when(jnp.logical_not(on_bottom))
        def _():
            to_north.wait_recv()

    def end_halo(k):
        to_east, to_west, to_fold, to_north, to_south = halo_copies(k)
        to_east.wait_send()
        to_west.wait_send()
        to_north.wait_send()

        @pl.when(jnp.logical_not(on_bottom))
        def _():
            to_south.wait_send()

    def part_copy(which, shift):
        return remote(part_out.at[which], part_in.at[which, shift - 1],
                      part_send.at[which], part_recv.at[which], device(shift))

    def share(which, values):
        packed = jnp.zeros((1, 128), f32)
        for k, value in enumerate(values):
            packed = jnp.where(lane == k, value, packed)
        part_out[which] = packed

        def send(shift, carry):
            part_copy(which, shift).start()
            return carry

        lax.fori_loop(1, count, send, 0)
        return packed

    def gathered(which):
        whole = part_in.at[which]
        pltpu.make_async_copy(whole, whole, part_recv.at[which]).wait()
        return jnp.sum(part_in[which], axis=0)

    def dot(a, b):
        return jnp.sum(jnp.sum(a * b, axis=0, keepdims=True), axis=1, keepdims=True)

    def pick(packed, k):
        return packed[:, k:k + 1]

    send_halo(0)
    take_halo(0)
    coef_east.wait_recv()

    @pl.when(on_top)
    def _():
        coef_fold.wait_recv()

    @pl.when(jnp.logical_not(on_bottom))
    def _():
        coef_north.wait_recv()

    top_flag = jnp.where(on_top, 1, 0)
    is_top = jnp.full((1, cols), top_flag, jnp.int32) == 1
    north_c = north[...]
    coef_mirror = jnp.where(is_top, coef_rows[0], 0.0)
    fold_c = 0.5 * (north_c[rows - 1:] + mirrored(coef_mirror))
    north_c = jnp.where(
        row_ids == rows - 1, jnp.where(is_top, fold_c, north_c[rows - 1:]), north_c)
    west_c = jnp.where(
        col_ids == 0, upright(coef_cols_in[:1]), pltpu.roll(east_c, 1, 1))
    south_c = jnp.where(row_ids == 0, coef_rows[1][7:8], pltpu.roll(north_c, 1, 0))
    east_c, west_c = ocean * east_c, ocean * west_c
    north_c, south_c = ocean * north_c, ocean * south_c
    centre = diag[...] + ((east_c + west_c) + (north_c + south_c))

    def operate(k, field):
        masked = held[k]
        block = rows_in[k, NORTH]
        above = jnp.where(is_top, mirrored(block), block[:1])
        below = rows_in[k, SOUTH][7:8]
        east_v = jnp.where(col_ids == cols - 1, upright(cols_in[k, 1][:1]), pltpu.roll(masked, cols - 1, 1))
        west_v = jnp.where(col_ids == 0, upright(cols_in[k, 0][:1]), pltpu.roll(masked, 1, 1))
        north_v = jnp.where(row_ids == rows - 1, above, pltpu.roll(masked, rows - 1, 0))
        south_v = jnp.where(row_ids == 0, below, pltpu.roll(masked, 1, 0))
        return centre * field - (
            (east_c * east_v + west_c * west_v) + (north_c * north_v + south_c * south_v))

    v0 = rhs[...]
    image = operate(0, v0)
    held[1] = ocean * image
    send_halo(1)
    packed = share(0, (dot(v0, v0), dot(v0, image), dot(image, image)))
    take_halo(1)
    second = operate(1, image)
    packed = packed + gathered(0)
    norm = pick(packed, 0)
    shift = pick(packed, 1) / norm
    spread = pick(packed, 2) / norm - shift * shift
    sigma = jnp.sqrt(jnp.maximum(spread, 1e-4 * shift * shift))
    scale = 1.0 / sigma
    v1 = (image - shift * v0) * scale
    v2 = ((second - shift * image) * scale - shift * v1) * scale - v0
    held[2] = ocean * v2
    send_halo(2)
    take_halo(2)
    v3 = (operate(2, v2) - shift * v2) * scale - v1
    held[3] = ocean * v3
    send_halo(3)
    take_halo(3)
    v4 = (operate(3, v3) - shift * v3) * scale - v2

    basis = (v0, v1, v2, v3, v4)
    pairs = [(i, j) for j in range(ITERS + 1) for i in range(j + 1) if i < ITERS]
    packed = share(1, [dot(basis[i], basis[j]) for i, j in pairs])
    packed = packed + gathered(1)
    gram = {}
    for k, (i, j) in enumerate(pairs):
        gram[i, j] = gram[j, i] = pick(packed, k)

    def inner(a, b):
        total = None
        for i, x in enumerate(a):
            line = None
            for j, y in enumerate(b):
                term = gram[i, j] * y
                line = term if line is None else line + term
            total = x * line if total is None else total + x * line
        return total

    def image_of(a):
        out = []
        for k in range(len(a) + 1):
            term = shift * a[k] if k < len(a) else None
            for near in (k - 1, k + 1):
                if 0 <= near < len(a):
                    term = sigma * a[near] if term is None else term + sigma * a[near]
            out.append(term)
        return out

    one = jnp.ones((1, 1), f32)
    left, way, found = [one], [one], []
    rr = inner(left, left)
    for step in range(ITERS):
        along = image_of(way)
        alpha = rr / inner(way, along)
        found = [(found[k] + alpha * w) if k < len(found) else alpha * w for k, w in enumerate(way)]
        left = [(left[k] - alpha * a) if k < len(left) else -alpha * a for k, a in enumerate(along)]
        if step + 1 < ITERS:
            new = inner(left, left)
            ratio = new / rr
            way = [(left[k] + ratio * way[k]) if k < len(way) else left[k] for k in range(len(left))]
            rr = new

    def mix(weights):
        total = weights[0] * basis[0]
        for weight, vector in zip(weights[1:], basis[1:]):
            total = total + weight * vector
        return total

    sol_ref[...] = mix(found)
    res_ref[...] = mix(left)

    for k in range(ITERS):
        end_halo(k)
    coef_east.wait_send()
    coef_fold.wait_send()
    for which in range(2):
        whole = part_in.at[which]
        pltpu.make_async_copy(whole, whole, part_send.at[which]).wait()


def solution(mesh):
    lats, lons = mesh.shape["lat"], mesh.shape["lon"]
    count = lats * lons

    def local(right_side, diagonal, east_coef, north_coef, land_sea, fold_partner):
        rows, cols = right_side.shape
        block = lambda dtype=f32: pltpu.VMEM((rows, cols), dtype)
        dma = pltpu.SemaphoreType.DMA
        return pl.pallas_call(
            lambda *refs: kernel(lats, lons, *refs),
            out_shape=(jax.ShapeDtypeStruct((rows, cols), f32),) * 2,
            in_specs=[pl.BlockSpec(memory_space=pl.ANY)] * 6,
            out_specs=(pl.BlockSpec(memory_space=pltpu.VMEM),) * 2,
            scratch_shapes=[
                block(), block(), block(), block(), block(jnp.int32),
                pltpu.VMEM((1, cols), jnp.int32), dma((6,)),
                pltpu.VMEM((ITERS, rows, cols), f32),
                pltpu.VMEM((ITERS, 2, 8, rows), f32),
                pltpu.VMEM((ITERS, 2, 8, cols), f32),
                pltpu.VMEM((ITERS, 2, 8, rows), f32),
                pltpu.VMEM((8, rows), f32),
                pltpu.VMEM((2, 8, cols), f32),
                pltpu.VMEM((8, rows), f32),
                dma((ITERS, 4)), dma((ITERS, 4)), dma((2,)), dma((3,)),
                pltpu.VMEM((2, 1, 128), f32),
                pltpu.VMEM((2, count - 1, 1, 128), f32),
                dma((2,)), dma((2,)),
            ],
            compiler_params=pltpu.CompilerParams(collective_id=0, has_side_effects=True),
            name="cg",
        )(right_side, diagonal, east_coef, north_coef, land_sea, fold_partner.reshape(1, cols))

    placed = (P("lat", "lon"),) * 5 + (P("lon"),)
    return jax.shard_map(
        local, mesh=mesh, in_specs=placed,
        out_specs=(P("lat", "lon"), P("lat", "lon")), check_vma=False)
```

```python
import jax
import jax.numpy as jnp
from jax import lax
from jax.experimental import pallas as pl
from jax.experimental.pallas import tpu as pltpu
from jax.sharding import PartitionSpec as P

ITERS = 4
MESH = pl.DeviceIdType.MESH
NORTH, SOUTH, EAST, WEST = range(4)
f32 = jnp.float32


def kernel(lats, lons, rhs_hbm, diag_hbm, east_hbm, north_hbm, land_hbm, partner_hbm,
           v0_ref, v1_ref, v2_ref, v3_ref, v4_ref, mix_ref,
           rhs, diag, east, north, land, partner, load_sem,
           held, cols_out, rows_in, cols_in, coef_cols, coef_rows, coef_cols_in,
           send_sem, recv_sem, coef_send, coef_recv,
           part_out, part_in, part_send, part_recv):
    rows, cols = rhs.shape
    count = lats * lons
    lat, lon = lax.axis_index("lat"), lax.axis_index("lon")
    me = lat * lons + lon
    on_top, on_bottom = lat == lats - 1, lat == 0

    loads = [
        pltpu.make_async_copy(src, dst, load_sem.at[i])
        for i, (src, dst) in enumerate(
            ((rhs_hbm, rhs), (land_hbm, land), (east_hbm, east), (north_hbm, north),
             (partner_hbm, partner), (diag_hbm, diag)))
    ]
    for load in loads:
        load.start()

    barrier = pltpu.get_barrier_semaphore()

    def device(shift):
        other = lax.rem(me + shift, count)
        return (other // lons, lax.rem(other, lons))

    def greet(shift, carry):
        pl.semaphore_signal(barrier, inc=1, device_id=device(shift), device_id_type=MESH)
        return carry

    lax.fori_loop(1, count, greet, 0)

    east_id = (lat, lax.rem(lon + 1, lons))
    west_id = (lat, lax.rem(lon + lons - 1, lons))
    north_id = (lax.rem(lat + 1, lats), lon)
    south_id = (lax.rem(lat + lats - 1, lats), lon)
    fold_id = (lat, lons - 1 - lon)

    row_ids = lax.broadcasted_iota(jnp.int32, (rows, cols), 0)
    col_ids = lax.broadcasted_iota(jnp.int32, (rows, cols), 1)
    eye = lax.broadcasted_iota(jnp.int32, (rows, rows), 0) == lax.broadcasted_iota(
        jnp.int32, (rows, rows), 1)
    lane = lax.broadcasted_iota(jnp.int32, (1, 128), 1)

    def flat(column):
        return jnp.sum(jnp.where(eye, column, 0.0), axis=0, keepdims=True)

    def upright(row):
        return jnp.sum(jnp.where(eye, row, 0.0), axis=1, keepdims=True)

    for load in loads:
        load.wait()
    ocean = land[...].astype(f32)
    east_c = east[...]
    coef_cols[...] = jnp.broadcast_to(flat(east_c[:, cols - 1:]), (8, rows))
    held[0] = ocean * rhs[...]

    own = lax.rem(partner[...], cols)
    lower = jnp.broadcast_to(lax.rem(own, 128), (8, cols))
    panel = jnp.broadcast_to(own // 128, (8, cols))

    def mirrored(block):
        pieces = []
        for at in range(0, cols, 128):
            index = lower[:, at:at + 128]
            which = panel[:, at:at + 128]
            picked = jnp.zeros((8, 128), f32)
            for k in range(cols // 128):
                found = jnp.take_along_axis(block[:, k * 128:(k + 1) * 128], index, axis=1)
                picked = jnp.where(which == k, found, picked)
            pieces.append(picked)
        return jnp.concatenate(pieces, axis=1)[7:8]

    @pl.when(on_bottom)
    def _():
        for k in range(ITERS):
            rows_in[k, SOUTH] = jnp.zeros((8, cols), f32)
        coef_rows[1] = jnp.zeros((8, cols), f32)

    pl.semaphore_wait(barrier, count - 1)

    def remote(src, dst, send, recv, to):
        return pltpu.make_async_remote_copy(
            src_ref=src, dst_ref=dst, send_sem=send, recv_sem=recv,
            device_id=to, device_id_type=MESH)

    def halo_copies(k):
        top, base = held.at[k, pl.ds(rows - 8, 8)], held.at[k, pl.ds(0, 8)]
        sems = lambda way: (send_sem.at[k, way], recv_sem.at[k, way])
        to_east = remote(cols_out.at[k, 0], cols_in.at[k, 0], *sems(WEST), east_id)
        to_west = remote(cols_out.at[k, 1], cols_in.at[k, 1], *sems(EAST), west_id)
        to_fold = remote(top, rows_in.at[k, NORTH], *sems(NORTH), fold_id)
        to_north = remote(top, rows_in.at[k, SOUTH], send_sem.at[k, NORTH], recv_sem.at[k, SOUTH], north_id)
        to_south = remote(base, rows_in.at[k, NORTH], send_sem.at[k, SOUTH], recv_sem.at[k, NORTH], south_id)
        return to_east, to_west, to_fold, to_north, to_south

    coef_east = remote(coef_cols, coef_cols_in, coef_send.at[0], coef_recv.at[0], east_id)
    coef_top = north.at[pl.ds(rows - 8, 8)]
    coef_fold = remote(coef_top, coef_rows.at[0], coef_send.at[1], coef_recv.at[1], fold_id)
    coef_north = remote(coef_top, coef_rows.at[1], coef_send.at[1], coef_recv.at[2], north_id)

    coef_east.start()

    @pl.when(on_top)
    def _():
        coef_fold.start()

    @pl.when(jnp.logical_not(on_top))
    def _():
        coef_north.start()

    def send_halo(k):
        to_east, to_west, to_fold, to_north, to_south = halo_copies(k)

        @pl.when(on_top)
        def _():
            to_fold.start()

        @pl.when(jnp.logical_not(on_top))
        def _():
            to_north.start()

        @pl.when(jnp.logical_not(on_bottom))
        def _():
            to_south.start()

        masked = held[k]
        cols_out[k, 0] = jnp.broadcast_to(flat(masked[:, cols - 1:]), (8, rows))
        cols_out[k, 1] = jnp.broadcast_to(flat(masked[:, :1]), (8, rows))
        to_east.start()
        to_west.start()

    def take_halo(k):
        to_east, to_west, to_fold, to_north, to_south = halo_copies(k)
        to_east.wait_recv()
        to_west.wait_recv()
        to_south.wait_recv()

        @pl.when(jnp.logical_not(on_bottom))
        def _():
            to_north.wait_recv()

    def end_halo(k):
        to_east, to_west, to_fold, to_north, to_south = halo_copies(k)
        to_east.wait_send()
        to_west.wait_send()
        to_north.wait_send()

        @pl.when(jnp.logical_not(on_bottom))
        def _():
            to_south.wait_send()

    def part_copy(which, shift):
        return remote(part_out.at[which], part_in.at[which, shift - 1],
                      part_send.at[which], part_recv.at[which], device(shift))

    def share(which, values):
        packed = jnp.zeros((1, 128), f32)
        for k, value in enumerate(values):
            packed = jnp.where(lane == k, value, packed)
        part_out[which] = packed

        def send(shift, carry):
            part_copy(which, shift).start()
            return carry

        lax.fori_loop(1, count, send, 0)
        return packed

    def gathered(which):
        whole = part_in.at[which]
        pltpu.make_async_copy(whole, whole, part_recv.at[which]).wait()
        return jnp.sum(part_in[which], axis=0)

    def dot(a, b):
        return jnp.sum(jnp.sum(a * b, axis=0, keepdims=True), axis=1, keepdims=True)

    def pick(packed, k):
        return packed[:, k:k + 1]

    send_halo(0)
    take_halo(0)
    coef_east.wait_recv()

    @pl.when(on_top)
    def _():
        coef_fold.wait_recv()

    @pl.when(jnp.logical_not(on_bottom))
    def _():
        coef_north.wait_recv()

    top_flag = jnp.where(on_top, 1, 0)
    is_top = jnp.full((1, cols), top_flag, jnp.int32) == 1
    north_c = north[...]
    coef_mirror = jnp.where(is_top, coef_rows[0], 0.0)
    fold_c = 0.5 * (north_c[rows - 1:] + mirrored(coef_mirror))
    north_c = jnp.where(
        row_ids == rows - 1, jnp.where(is_top, fold_c, north_c[rows - 1:]), north_c)
    west_c = jnp.where(
        col_ids == 0, upright(coef_cols_in[:1]), pltpu.roll(east_c, 1, 1))
    south_c = jnp.where(row_ids == 0, coef_rows[1][7:8], pltpu.roll(north_c, 1, 0))
    east_c, west_c = ocean * east_c, ocean * west_c
    north_c, south_c = ocean * north_c, ocean * south_c
    centre = diag[...] + ((east_c + west_c) + (north_c + south_c))

    def operate(k, field):
        masked = held[k]
        block = rows_in[k, NORTH]
        above = jnp.where(is_top, mirrored(block), block[:1])
        below = rows_in[k, SOUTH][7:8]
        east_v = jnp.where(col_ids == cols - 1, upright(cols_in[k, 1][:1]), pltpu.roll(masked, cols - 1, 1))
        west_v = jnp.where(col_ids == 0, upright(cols_in[k, 0][:1]), pltpu.roll(masked, 1, 1))
        north_v = jnp.where(row_ids == rows - 1, above, pltpu.roll(masked, rows - 1, 0))
        south_v = jnp.where(row_ids == 0, below, pltpu.roll(masked, 1, 0))
        return centre * field - (
            (east_c * east_v + west_c * west_v) + (north_c * north_v + south_c * south_v))

    v0 = rhs[...]
    image = operate(0, v0)
    held[1] = ocean * image
    send_halo(1)
    packed = share(0, (dot(v0, v0), dot(v0, image), dot(image, image)))
    take_halo(1)
    second = operate(1, image)
    packed = packed + gathered(0)
    norm = pick(packed, 0)
    shift = pick(packed, 1) / norm
    spread = pick(packed, 2) / norm - shift * shift
    sigma = jnp.sqrt(jnp.maximum(spread, 1e-4 * shift * shift))
    scale = 1.0 / sigma
    v1 = (image - shift * v0) * scale
    v2 = ((second - shift * image) * scale - shift * v1) * scale - v0
    held[2] = ocean * v2
    send_halo(2)
    take_halo(2)
    v3 = (operate(2, v2) - shift * v2) * scale - v1
    held[3] = ocean * v3
    send_halo(3)
    take_halo(3)
    v4 = (operate(3, v3) - shift * v3) * scale - v2
    v0_ref[...] = v0
    v1_ref[...] = v1
    v2_ref[...] = v2
    v3_ref[...] = v3
    v4_ref[...] = v4

    basis = (v0, v1, v2, v3, v4)
    pairs = [(i, j) for j in range(ITERS + 1) for i in range(j + 1) if i < ITERS]
    packed = share(1, [dot(basis[i], basis[j]) for i, j in pairs])
    packed = packed + gathered(1)
    gram = {}
    for k, (i, j) in enumerate(pairs):
        gram[i, j] = gram[j, i] = pick(packed, k)

    def inner(a, b):
        total = None
        for i, x in enumerate(a):
            line = None
            for j, y in enumerate(b):
                term = gram[i, j] * y
                line = term if line is None else line + term
            total = x * line if total is None else total + x * line
        return total

    def image_of(a):
        out = []
        for k in range(len(a) + 1):
            term = shift * a[k] if k < len(a) else None
            for near in (k - 1, k + 1):
                if 0 <= near < len(a):
                    term = sigma * a[near] if term is None else term + sigma * a[near]
            out.append(term)
        return out

    one = jnp.ones((1, 1), f32)
    left, way, found = [one], [one], []
    rr = inner(left, left)
    for step in range(ITERS):
        along = image_of(way)
        alpha = rr / inner(way, along)
        found = [(found[k] + alpha * w) if k < len(found) else alpha * w for k, w in enumerate(way)]
        left = [(left[k] - alpha * a) if k < len(left) else -alpha * a for k, a in enumerate(along)]
        if step + 1 < ITERS:
            new = inner(left, left)
            ratio = new / rr
            way = [(left[k] + ratio * way[k]) if k < len(way) else left[k] for k in range(len(left))]
            rr = new

    weights = jnp.zeros((8, 128), f32)
    spot = 128 * lax.broadcasted_iota(jnp.int32, (8, 128), 0) + lax.broadcasted_iota(
        jnp.int32, (8, 128), 1)
    for k, weight in enumerate(found):
        weights = jnp.where(spot == k, weight, weights)
    for k, weight in enumerate(left):
        weights = jnp.where(spot == 128 + k, weight, weights)
    mix_ref[...] = weights

    for k in range(ITERS):
        end_halo(k)
    coef_east.wait_send()
    coef_fold.wait_send()
    for which in range(2):
        whole = part_in.at[which]
        pltpu.make_async_copy(whole, whole, part_send.at[which]).wait()


def combine(v0_ref, v1_ref, v2_ref, v3_ref, v4_ref, mix_ref, sol_ref, res_ref):
    basis = [ref[...] for ref in (v0_ref, v1_ref, v2_ref, v3_ref, v4_ref)]
    for line, size, out_ref in ((0, ITERS, sol_ref), (1, ITERS + 1, res_ref)):
        total = mix_ref[line:line + 1, 0:1] * basis[0]
        for k in range(1, size):
            total = total + mix_ref[line:line + 1, k:k + 1] * basis[k]
        out_ref[...] = total


def solution(mesh):
    lats, lons = mesh.shape["lat"], mesh.shape["lon"]
    count = lats * lons

    def local(right_side, diagonal, east_coef, north_coef, land_sea, fold_partner):
        rows, cols = right_side.shape
        block = lambda dtype=f32: pltpu.VMEM((rows, cols), dtype)
        dma = pltpu.SemaphoreType.DMA
        *basis, weights = pl.pallas_call(
            lambda *refs: kernel(lats, lons, *refs),
            out_shape=(pltpu.VMEM((rows, cols), f32),) * (ITERS + 1) + (pltpu.VMEM((8, 128), f32),),
            in_specs=[pl.BlockSpec(memory_space=pl.ANY)] * 6,
            out_specs=(pl.BlockSpec(memory_space=pltpu.VMEM),) * (ITERS + 2),
            scratch_shapes=[
                block(), block(), block(), block(), block(jnp.int32),
                pltpu.VMEM((1, cols), jnp.int32), dma((6,)),
                pltpu.VMEM((ITERS, rows, cols), f32),
                pltpu.VMEM((ITERS, 2, 8, rows), f32),
                pltpu.VMEM((ITERS, 2, 8, cols), f32),
                pltpu.VMEM((ITERS, 2, 8, rows), f32),
                pltpu.VMEM((8, rows), f32),
                pltpu.VMEM((2, 8, cols), f32),
                pltpu.VMEM((8, rows), f32),
                dma((ITERS, 4)), dma((ITERS, 4)), dma((2,)), dma((3,)),
                pltpu.VMEM((2, 1, 128), f32),
                pltpu.VMEM((2, count - 1, 1, 128), f32),
                dma((2,)), dma((2,)),
            ],
            compiler_params=pltpu.CompilerParams(collective_id=0, has_side_effects=True),
            name="cg",
        )(right_side, diagonal, east_coef, north_coef, land_sea, fold_partner.reshape(1, cols))

        return pl.pallas_call(
            combine,
            out_shape=(jax.ShapeDtypeStruct((rows, cols), f32),) * 2,
            in_specs=[pl.BlockSpec(memory_space=pltpu.VMEM)] * (ITERS + 2),
            out_specs=(pl.BlockSpec(memory_space=pltpu.VMEM),) * 2,
            name="combine",
        )(*[pltpu.with_memory_space_constraint(x, pltpu.VMEM) for x in (*basis, weights)])

    placed = (P("lat", "lon"),) * 5 + (P("lon"),)
    return jax.shard_map(
        local, mesh=mesh, in_specs=placed,
        out_specs=(P("lat", "lon"), P("lat", "lon")), check_vma=False)
```

```python
import jax
import jax.numpy as jnp
from jax import lax
from jax.experimental import pallas as pl
from jax.experimental.pallas import tpu as pltpu
from jax.sharding import PartitionSpec as P

ITERS = 4
MESH = pl.DeviceIdType.MESH
NORTH, SOUTH, EAST, WEST = range(4)
f32 = jnp.float32


def kernel(lats, lons, rhs_hbm, diag_hbm, east_hbm, north_hbm, land_hbm, partner_hbm,
           v0_ref, v1_ref, v2_ref, v3_ref, v4_ref, mix_ref,
           rhs, diag, east, north, land, partner, load_sem,
           held, cols_out, rows_in, cols_in, coef_cols, coef_rows, coef_cols_in,
           send_sem, recv_sem, coef_send, coef_recv,
           part_out, part_in, part_send, part_recv):
    rows, cols = rhs.shape
    count = lats * lons
    lat, lon = lax.axis_index("lat"), lax.axis_index("lon")
    me = lat * lons + lon
    on_top, on_bottom = lat == lats - 1, lat == 0

    loads = [
        pltpu.make_async_copy(src, dst, load_sem.at[i])
        for i, (src, dst) in enumerate(
            ((rhs_hbm, rhs), (land_hbm, land), (east_hbm, east), (north_hbm, north),
             (partner_hbm, partner), (diag_hbm, diag)))
    ]
    for load in loads:
        load.start()

    barrier = pltpu.get_barrier_semaphore()

    def device(shift):
        other = lax.rem(me + shift, count)
        return (other // lons, lax.rem(other, lons))

    def greet(shift, carry):
        pl.semaphore_signal(barrier, inc=1, device_id=device(shift), device_id_type=MESH)
        return carry

    lax.fori_loop(1, count, greet, 0)

    east_id = (lat, lax.rem(lon + 1, lons))
    west_id = (lat, lax.rem(lon + lons - 1, lons))
    north_id = (lax.rem(lat + 1, lats), lon)
    south_id = (lax.rem(lat + lats - 1, lats), lon)
    fold_id = (lat, lons - 1 - lon)

    row_ids = lax.broadcasted_iota(jnp.int32, (rows, cols), 0)
    col_ids = lax.broadcasted_iota(jnp.int32, (rows, cols), 1)
    eye = lax.broadcasted_iota(jnp.int32, (rows, rows), 0) == lax.broadcasted_iota(
        jnp.int32, (rows, rows), 1)
    lane = lax.broadcasted_iota(jnp.int32, (1, 128), 1)

    def flat(column):
        return jnp.sum(jnp.where(eye, column, 0.0), axis=0, keepdims=True)

    def upright(row):
        return jnp.sum(jnp.where(eye, row, 0.0), axis=1, keepdims=True)

    for load in loads:
        load.wait()
    ocean = land[...].astype(f32)
    east_c = east[...]
    coef_cols[...] = jnp.broadcast_to(flat(east_c[:, cols - 1:]), (8, rows))
    v0 = rhs[...]
    masked = ocean * v0
    held[0] = masked
    north_c = north[...]

    def rolled(field):
        return (pltpu.roll(field, cols - 1, 1), pltpu.roll(field, 1, 1),
                pltpu.roll(field, rows - 1, 0), pltpu.roll(field, 1, 0))

    def dot(a, b):
        return jnp.sum(jnp.sum(a * b, axis=0, keepdims=True), axis=1, keepdims=True)

    def pick(packed, k):
        return packed[:, k:k + 1]

    def pack(values):
        packed = jnp.zeros((1, 128), f32)
        for k, value in enumerate(values):
            packed = jnp.where(lane == k, value, packed)
        return packed

    west_raw, south_raw = pltpu.roll(east_c, 1, 1), pltpu.roll(north_c, 1, 0)
    guess = diag[...] * v0
    for coef, other in zip((east_c, west_raw, north_c, south_raw), rolled(masked)):
        guess = guess + ocean * (coef * (masked - other))
    guessed = pack((dot(v0, v0), dot(v0, guess), dot(guess, guess)))
    part_out[0] = guessed

    own = lax.rem(partner[...], cols)
    lower = jnp.broadcast_to(lax.rem(own, 128), (8, cols))
    panel = jnp.broadcast_to(own // 128, (8, cols))

    def mirrored(block):
        pieces = []
        for at in range(0, cols, 128):
            index = lower[:, at:at + 128]
            which = panel[:, at:at + 128]
            picked = jnp.zeros((8, 128), f32)
            for k in range(cols // 128):
                found = jnp.take_along_axis(block[:, k * 128:(k + 1) * 128], index, axis=1)
                picked = jnp.where(which == k, found, picked)
            pieces.append(picked)
        return jnp.concatenate(pieces, axis=1)[7:8]

    @pl.when(on_bottom)
    def _():
        for k in range(ITERS):
            rows_in[k, SOUTH] = jnp.zeros((8, cols), f32)
        coef_rows[1] = jnp.zeros((8, cols), f32)

    pl.semaphore_wait(barrier, count - 1)

    def remote(src, dst, send, recv, to):
        return pltpu.make_async_remote_copy(
            src_ref=src, dst_ref=dst, send_sem=send, recv_sem=recv,
            device_id=to, device_id_type=MESH)

    def halo_copies(k):
        top, base = held.at[k, pl.ds(rows - 8, 8)], held.at[k, pl.ds(0, 8)]
        sems = lambda way: (send_sem.at[k, way], recv_sem.at[k, way])
        to_east = remote(cols_out.at[k, 0], cols_in.at[k, 0], *sems(WEST), east_id)
        to_west = remote(cols_out.at[k, 1], cols_in.at[k, 1], *sems(EAST), west_id)
        to_fold = remote(top, rows_in.at[k, NORTH], *sems(NORTH), fold_id)
        to_north = remote(top, rows_in.at[k, SOUTH], send_sem.at[k, NORTH], recv_sem.at[k, SOUTH], north_id)
        to_south = remote(base, rows_in.at[k, NORTH], send_sem.at[k, SOUTH], recv_sem.at[k, NORTH], south_id)
        return to_east, to_west, to_fold, to_north, to_south

    coef_east = remote(coef_cols, coef_cols_in, coef_send.at[0], coef_recv.at[0], east_id)
    coef_top = north.at[pl.ds(rows - 8, 8)]
    coef_fold = remote(coef_top, coef_rows.at[0], coef_send.at[1], coef_recv.at[1], fold_id)
    coef_north = remote(coef_top, coef_rows.at[1], coef_send.at[1], coef_recv.at[2], north_id)

    coef_east.start()

    @pl.when(on_top)
    def _():
        coef_fold.start()

    @pl.when(jnp.logical_not(on_top))
    def _():
        coef_north.start()

    def send_halo(k):
        to_east, to_west, to_fold, to_north, to_south = halo_copies(k)

        @pl.when(on_top)
        def _():
            to_fold.start()

        @pl.when(jnp.logical_not(on_top))
        def _():
            to_north.start()

        @pl.when(jnp.logical_not(on_bottom))
        def _():
            to_south.start()

        masked = held[k]
        cols_out[k, 0] = jnp.broadcast_to(flat(masked[:, cols - 1:]), (8, rows))
        cols_out[k, 1] = jnp.broadcast_to(flat(masked[:, :1]), (8, rows))
        to_east.start()
        to_west.start()

    def take_halo(k):
        to_east, to_west, to_fold, to_north, to_south = halo_copies(k)
        to_east.wait_recv()
        to_west.wait_recv()
        to_south.wait_recv()

        @pl.when(jnp.logical_not(on_bottom))
        def _():
            to_north.wait_recv()

    def end_halo(k):
        to_east, to_west, to_fold, to_north, to_south = halo_copies(k)
        to_east.wait_send()
        to_west.wait_send()
        to_north.wait_send()

        @pl.when(jnp.logical_not(on_bottom))
        def _():
            to_south.wait_send()

    def part_copy(which, shift):
        return remote(part_out.at[which], part_in.at[which, shift - 1],
                      part_send.at[which], part_recv.at[which], device(shift))

    def share(which):
        def send(shift, carry):
            part_copy(which, shift).start()
            return carry

        lax.fori_loop(1, count, send, 0)

    def gathered(which):
        whole = part_in.at[which]
        pltpu.make_async_copy(whole, whole, part_recv.at[which]).wait()
        return jnp.sum(part_in[which], axis=0)

    send_halo(0)
    share(0)
    take_halo(0)
    coef_east.wait_recv()

    @pl.when(on_top)
    def _():
        coef_fold.wait_recv()

    @pl.when(jnp.logical_not(on_bottom))
    def _():
        coef_north.wait_recv()

    top_flag = jnp.where(on_top, 1, 0)
    is_top = jnp.full((1, cols), top_flag, jnp.int32) == 1
    coef_mirror = jnp.where(is_top, coef_rows[0], 0.0)
    fold_c = 0.5 * (north_c[rows - 1:] + mirrored(coef_mirror))
    north_c = jnp.where(
        row_ids == rows - 1, jnp.where(is_top, fold_c, north_c[rows - 1:]), north_c)
    west_c = ocean * jnp.where(col_ids == 0, upright(coef_cols_in[:1]), west_raw)
    south_c = ocean * jnp.where(row_ids == 0, coef_rows[1][7:8], south_raw)
    east_c, north_c = ocean * east_c, ocean * north_c
    centre = diag[...] + ((east_c + west_c) + (north_c + south_c))
    last_panel = slice(cols - 128, cols)
    east_edge = jnp.where(col_ids == cols - 1, east_c, 0.0)[:, last_panel]
    west_edge = jnp.where(col_ids == 0, west_c, 0.0)[:, :128]
    north_edge, south_edge = north_c[rows - 1:], south_c[:1]
    inside = (jnp.where(col_ids == cols - 1, 0.0, east_c),
              jnp.where(col_ids == 0, 0.0, west_c),
              jnp.where(row_ids == rows - 1, 0.0, north_c),
              jnp.where(row_ids == 0, 0.0, south_c))
    base_row = jnp.where(row_ids == 0, 1.0, 0.0)[:8]
    top_row = jnp.where(row_ids == rows - 1, 1.0, 0.0)[rows - 8:]

    def interior(k, field):
        terms = [coef * other for coef, other in zip(inside, rolled(held[k]))]
        return centre * field - ((terms[0] + terms[1]) + (terms[2] + terms[3]))

    def with_edges(k, image):
        block = rows_in[k, NORTH]
        above = jnp.where(is_top, mirrored(block), block[:1])
        below = rows_in[k, SOUTH][7:8]
        image = jnp.concatenate([
            image[:8] - base_row * (south_edge * below),
            image[8:rows - 8],
            image[rows - 8:] - top_row * (north_edge * above)], axis=0)
        return jnp.concatenate([
            image[:, :128] - west_edge * upright(cols_in[k, 0][:1]),
            *([image[:, 128:cols - 128]] if cols > 256 else []),
            image[:, last_panel] - east_edge * upright(cols_in[k, 1][:1])], axis=1)

    image = with_edges(0, interior(0, v0))
    held[1] = ocean * image
    send_halo(1)
    packed = guessed + gathered(0)
    norm = pick(packed, 0)
    shift = pick(packed, 1) / norm
    spread = pick(packed, 2) / norm - shift * shift
    sigma = jnp.sqrt(jnp.maximum(spread, 1e-4 * shift * shift))
    scale = 1.0 / sigma
    v1 = (image - shift * v0) * scale
    second = interior(1, image) - shift * image
    v0_ref[...] = v0
    v1_ref[...] = v1
    base2 = (second * scale - shift * v1) * scale - v0
    early = [dot(v0, v0), dot(v0, v1)]
    take_halo(1)
    v2 = base2 + with_edges(1, jnp.zeros_like(v0)) * (scale * scale)
    held[2] = ocean * v2
    send_halo(2)
    v2_ref[...] = v2
    base3 = (interior(2, v2) - shift * v2) * scale - v1
    early += [dot(v0, v2), dot(v2, v2)]
    take_halo(2)
    v3 = base3 + with_edges(2, jnp.zeros_like(v0)) * scale
    held[3] = ocean * v3
    send_halo(3)
    v3_ref[...] = v3
    base4 = (interior(3, v3) - shift * v3) * scale - v2
    early += [dot(v0, v3), dot(v2, v3), dot(v3, v3)]
    early = pack(early)
    take_halo(3)
    v4 = base4 + with_edges(3, jnp.zeros_like(v0)) * scale
    packed = jnp.where(lane == 7, dot(v3, v4), early)
    part_out[1] = packed
    share(1)
    v4_ref[...] = v4
    packed = packed + gathered(1)

    p00, p01, p02, p22, p03, p23, p33, p34 = [pick(packed, k) for k in range(8)]
    moment = [p00, p01, p02, p03, p22 - p00 - p02, p23 - p01 - p03]
    moment.append(p33 - p00 - p02 - moment[4])
    moment.append(p34 - p01 - p03 - moment[5])
    gram = {}
    for i in range(ITERS + 1):
        for j in range(i, ITERS + 1):
            if i + j < 2 * ITERS:
                gram[i, j] = gram[j, i] = sum(moment[k] for k in range(j - i, i + j + 1, 2))

    def inner(a, b):
        total = None
        for i, x in enumerate(a):
            line = None
            for j, y in enumerate(b):
                term = gram[i, j] * y
                line = term if line is None else line + term
            total = x * line if total is None else total + x * line
        return total

    def image_of(a):
        out = []
        for k in range(len(a) + 1):
            term = shift * a[k] if k < len(a) else None
            for near in (k - 1, k + 1):
                if 0 <= near < len(a):
                    term = sigma * a[near] if term is None else term + sigma * a[near]
            out.append(term)
        return out

    one = jnp.ones((1, 1), f32)
    left, way, found = [one], [one], []
    rr = inner(left, left)
    for step in range(ITERS):
        along = image_of(way)
        alpha = rr / inner(way, along)
        found = [(found[k] + alpha * w) if k < len(found) else alpha * w for k, w in enumerate(way)]
        left = [(left[k] - alpha * a) if k < len(left) else -alpha * a for k, a in enumerate(along)]
        if step + 1 < ITERS:
            new = inner(left, left)
            ratio = new / rr
            way = [(left[k] + ratio * way[k]) if k < len(way) else left[k] for k in range(len(left))]
            rr = new

    weights = jnp.zeros((8, 128), f32)
    spot = 128 * lax.broadcasted_iota(jnp.int32, (8, 128), 0) + lax.broadcasted_iota(
        jnp.int32, (8, 128), 1)
    for k, weight in enumerate(found):
        weights = jnp.where(spot == k, weight, weights)
    for k, weight in enumerate(left):
        weights = jnp.where(spot == 128 + k, weight, weights)
    mix_ref[...] = weights

    for k in range(ITERS):
        end_halo(k)
    coef_east.wait_send()
    coef_fold.wait_send()
    for which in range(2):
        whole = part_in.at[which]
        pltpu.make_async_copy(whole, whole, part_send.at[which]).wait()


def combine(v0_ref, v1_ref, v2_ref, v3_ref, v4_ref, mix_ref, sol_ref, res_ref):
    basis = [ref[...] for ref in (v0_ref, v1_ref, v2_ref, v3_ref, v4_ref)]
    for line, size, out_ref in ((0, ITERS, sol_ref), (1, ITERS + 1, res_ref)):
        total = mix_ref[line:line + 1, 0:1] * basis[0]
        for k in range(1, size):
            total = total + mix_ref[line:line + 1, k:k + 1] * basis[k]
        out_ref[...] = total


def solution(mesh):
    lats, lons = mesh.shape["lat"], mesh.shape["lon"]
    count = lats * lons

    def local(right_side, diagonal, east_coef, north_coef, land_sea, fold_partner):
        rows, cols = right_side.shape
        block = lambda dtype=f32: pltpu.VMEM((rows, cols), dtype)
        dma = pltpu.SemaphoreType.DMA
        *basis, weights = pl.pallas_call(
            lambda *refs: kernel(lats, lons, *refs),
            out_shape=(pltpu.VMEM((rows, cols), f32),) * (ITERS + 1) + (pltpu.VMEM((8, 128), f32),),
            in_specs=[pl.BlockSpec(memory_space=pl.ANY)] * 6,
            out_specs=(pl.BlockSpec(memory_space=pltpu.VMEM),) * (ITERS + 2),
            scratch_shapes=[
                block(), block(), block(), block(), block(jnp.int32),
                pltpu.VMEM((1, cols), jnp.int32), dma((6,)),
                pltpu.VMEM((ITERS, rows, cols), f32),
                pltpu.VMEM((ITERS, 2, 8, rows), f32),
                pltpu.VMEM((ITERS, 2, 8, cols), f32),
                pltpu.VMEM((ITERS, 2, 8, rows), f32),
                pltpu.VMEM((8, rows), f32),
                pltpu.VMEM((2, 8, cols), f32),
                pltpu.VMEM((8, rows), f32),
                dma((ITERS, 4)), dma((ITERS, 4)), dma((2,)), dma((3,)),
                pltpu.VMEM((2, 1, 128), f32),
                pltpu.VMEM((2, count - 1, 1, 128), f32),
                dma((2,)), dma((2,)),
            ],
            compiler_params=pltpu.CompilerParams(collective_id=0, has_side_effects=True),
            name="cg",
        )(right_side, diagonal, east_coef, north_coef, land_sea, fold_partner.reshape(1, cols))

        return pl.pallas_call(
            combine,
            out_shape=(jax.ShapeDtypeStruct((rows, cols), f32),) * 2,
            in_specs=[pl.BlockSpec(memory_space=pltpu.VMEM)] * (ITERS + 2),
            out_specs=(pl.BlockSpec(memory_space=pltpu.VMEM),) * 2,
            name="combine",
        )(*[pltpu.with_memory_space_constraint(x, pltpu.VMEM) for x in (*basis, weights)])

    placed = (P("lat", "lon"),) * 5 + (P("lon"),)
    return jax.shard_map(
        local, mesh=mesh, in_specs=placed,
        out_specs=(P("lat", "lon"), P("lat", "lon")), check_vma=False)
```

```python
import jax
import jax.numpy as jnp
from jax import lax
from jax.experimental import pallas as pl
from jax.experimental.pallas import tpu as pltpu
from jax.sharding import PartitionSpec as P

ITERS = 4
MESH = pl.DeviceIdType.MESH
NORTH, SOUTH, EAST, WEST = range(4)
f32 = jnp.float32


def kernel(lats, lons, rhs_hbm, diag_hbm, east_hbm, north_hbm, land_hbm, partner_hbm,
           v0_ref, v1_ref, v2_ref, v3_ref, v4_ref, mix_ref,
           rhs, diag, east, north, land, partner, load_sem,
           held, cols_out, rows_in, cols_in, coef_cols, coef_rows, coef_cols_in,
           send_sem, recv_sem, coef_send, coef_recv,
           part_out, part_in, part_send, part_recv, all_in,
           guess_out, row_in, column_in, guess_send, guess_recv):
    rows, cols = rhs.shape
    lat, lon = lax.axis_index("lat"), lax.axis_index("lon")
    on_top, on_bottom = lat == lats - 1, lat == 0

    loads = [
        pltpu.make_async_copy(src, dst, load_sem.at[i])
        for i, (src, dst) in enumerate(
            ((rhs_hbm, rhs), (land_hbm, land), (east_hbm, east), (north_hbm, north),
             (partner_hbm, partner), (diag_hbm, diag)))
    ]
    for load in loads:
        load.start()

    barrier = pltpu.get_barrier_semaphore()

    def greet_lat(step, carry):
        pl.semaphore_signal(barrier, inc=1, device_id=(lax.rem(lat + step, lats), lon), device_id_type=MESH)
        return carry

    def greet_lon(step, carry):
        pl.semaphore_signal(barrier, inc=1, device_id=(lat, lax.rem(lon + step, lons)), device_id_type=MESH)
        return carry

    def pass_on(step, carry):
        pl.semaphore_signal(all_in, inc=1, device_id=(lat, lax.rem(lon + step, lons)), device_id_type=MESH)
        return carry

    lax.fori_loop(1, lons, greet_lon, 0)
    lax.fori_loop(1, lats, greet_lat, 0)

    east_id = (lat, lax.rem(lon + 1, lons))
    west_id = (lat, lax.rem(lon + lons - 1, lons))
    north_id = (lax.rem(lat + 1, lats), lon)
    south_id = (lax.rem(lat + lats - 1, lats), lon)
    fold_id = (lat, lons - 1 - lon)

    row_ids = lax.broadcasted_iota(jnp.int32, (rows, cols), 0)
    col_ids = lax.broadcasted_iota(jnp.int32, (rows, cols), 1)
    eye = lax.broadcasted_iota(jnp.int32, (rows, rows), 0) == lax.broadcasted_iota(
        jnp.int32, (rows, rows), 1)
    lane = lax.broadcasted_iota(jnp.int32, (1, 128), 1)

    def flat(column):
        return jnp.sum(jnp.where(eye, column, 0.0), axis=0, keepdims=True)

    def upright(row):
        return jnp.sum(jnp.where(eye, row, 0.0), axis=1, keepdims=True)

    for load in loads:
        load.wait()
    ocean = land[...].astype(f32)
    east_c = east[...]
    coef_cols[...] = jnp.broadcast_to(flat(east_c[:, cols - 1:]), (8, rows))
    v0 = rhs[...]
    masked = ocean * v0
    held[0] = masked
    north_c = north[...]

    def rolled(field):
        return (pltpu.roll(field, cols - 1, 1), pltpu.roll(field, 1, 1),
                pltpu.roll(field, rows - 1, 0), pltpu.roll(field, 1, 0))

    def dot(a, b):
        return jnp.sum(jnp.sum(a * b, axis=0, keepdims=True), axis=1, keepdims=True)

    def pick(packed, k):
        return packed[:, k:k + 1]

    def pack(values):
        packed = jnp.zeros((1, 128), f32)
        for k, value in enumerate(values):
            packed = jnp.where(lane == k, value, packed)
        return packed

    west_raw, south_raw = pltpu.roll(east_c, 1, 1), pltpu.roll(north_c, 1, 0)
    guess = diag[...] * v0
    for coef, other in zip((east_c, west_raw, north_c, south_raw), rolled(masked)):
        guess = guess + ocean * (coef * (masked - other))
    guessed = pack((dot(v0, v0), dot(v0, guess), dot(guess, guess)))
    guess_out[0] = guessed

    own = lax.rem(partner[...], cols)
    lower = jnp.broadcast_to(lax.rem(own, 128), (8, cols))
    panel = jnp.broadcast_to(own // 128, (8, cols))

    def mirrored(block):
        pieces = []
        for at in range(0, cols, 128):
            index = lower[:, at:at + 128]
            which = panel[:, at:at + 128]
            picked = jnp.zeros((8, 128), f32)
            for k in range(cols // 128):
                found = jnp.take_along_axis(block[:, k * 128:(k + 1) * 128], index, axis=1)
                picked = jnp.where(which == k, found, picked)
            pieces.append(picked)
        return jnp.concatenate(pieces, axis=1)[7:8]

    @pl.when(on_bottom)
    def _():
        for k in range(ITERS):
            rows_in[k, SOUTH] = jnp.zeros((8, cols), f32)
        coef_rows[1] = jnp.zeros((8, cols), f32)

    pl.semaphore_wait(barrier, lats + lons - 2)

    def remote(src, dst, send, recv, to):
        return pltpu.make_async_remote_copy(
            src_ref=src, dst_ref=dst, send_sem=send, recv_sem=recv,
            device_id=to, device_id_type=MESH)

    def halo_copies(k):
        top, base = held.at[k, pl.ds(rows - 8, 8)], held.at[k, pl.ds(0, 8)]
        sems = lambda way: (send_sem.at[k, way], recv_sem.at[k, way])
        to_east = remote(cols_out.at[k, 0], cols_in.at[k, 0], *sems(WEST), east_id)
        to_west = remote(cols_out.at[k, 1], cols_in.at[k, 1], *sems(EAST), west_id)
        to_fold = remote(top, rows_in.at[k, NORTH], *sems(NORTH), fold_id)
        to_north = remote(top, rows_in.at[k, SOUTH], send_sem.at[k, NORTH], recv_sem.at[k, SOUTH], north_id)
        to_south = remote(base, rows_in.at[k, NORTH], send_sem.at[k, SOUTH], recv_sem.at[k, NORTH], south_id)
        return to_east, to_west, to_fold, to_north, to_south

    coef_east = remote(coef_cols, coef_cols_in, coef_send.at[0], coef_recv.at[0], east_id)
    coef_top = north.at[pl.ds(rows - 8, 8)]
    coef_fold = remote(coef_top, coef_rows.at[0], coef_send.at[1], coef_recv.at[1], fold_id)
    coef_north = remote(coef_top, coef_rows.at[1], coef_send.at[1], coef_recv.at[2], north_id)

    coef_east.start()

    @pl.when(on_top)
    def _():
        coef_fold.start()

    @pl.when(jnp.logical_not(on_top))
    def _():
        coef_north.start()

    def send_halo(k):
        to_east, to_west, to_fold, to_north, to_south = halo_copies(k)

        @pl.when(on_top)
        def _():
            to_fold.start()

        @pl.when(jnp.logical_not(on_top))
        def _():
            to_north.start()

        @pl.when(jnp.logical_not(on_bottom))
        def _():
            to_south.start()

        masked = held[k]
        cols_out[k, 0] = jnp.broadcast_to(flat(masked[:, cols - 1:]), (8, rows))
        cols_out[k, 1] = jnp.broadcast_to(flat(masked[:, :1]), (8, rows))
        to_east.start()
        to_west.start()

    def take_halo(k):
        to_east, to_west, to_fold, to_north, to_south = halo_copies(k)
        to_east.wait_recv()
        to_west.wait_recv()
        to_south.wait_recv()

        @pl.when(jnp.logical_not(on_bottom))
        def _():
            to_north.wait_recv()

    def end_halo(k):
        to_east, to_west, to_fold, to_north, to_south = halo_copies(k)
        to_east.wait_send()
        to_west.wait_send()
        to_north.wait_send()

        @pl.when(jnp.logical_not(on_bottom))
        def _():
            to_south.wait_send()

    def lon_at(step):
        return (lat, lax.rem(lon + step, lons))

    def lat_at(step):
        return (lax.rem(lat + step, lats), lon)

    def row_copy(step):
        return remote(guess_out.at[0], row_in.at[step - 1], guess_send.at[0], guess_recv.at[0], lon_at(step))

    def column_copy(step):
        return remote(guess_out.at[1], column_in.at[step - 1], guess_send.at[1], guess_recv.at[1], lat_at(step))

    def part_copy(up, right):
        to = (lax.rem(lat + up, lats), lax.rem(lon + right, lons))
        return remote(part_out, part_in.at[up * lons + right - 1], part_send.at[0], part_recv.at[0], to)

    def start_row(step, carry):
        row_copy(step).start()
        return carry

    def start_column(step, carry):
        column_copy(step).start()
        return carry

    def await_all(whole, sem):
        pltpu.make_async_copy(whole, whole, sem).wait()

    def share():
        for up in reversed(range(lats)):
            def send(right, carry):
                part_copy(up, right).start()
                return carry

            lax.fori_loop(0 if up else 1, lons, send, 0)

    send_halo(0)
    lax.fori_loop(1, lons, start_row, 0)
    lax.fori_loop(1, lons, pass_on, 0)
    take_halo(0)
    coef_east.wait_recv()

    @pl.when(on_top)
    def _():
        coef_fold.wait_recv()

    @pl.when(jnp.logical_not(on_bottom))
    def _():
        coef_north.wait_recv()

    top_flag = jnp.where(on_top, 1, 0)
    is_top = jnp.full((1, cols), top_flag, jnp.int32) == 1
    coef_mirror = jnp.where(is_top, coef_rows[0], 0.0)
    fold_c = 0.5 * (north_c[rows - 1:] + mirrored(coef_mirror))
    north_c = jnp.where(
        row_ids == rows - 1, jnp.where(is_top, fold_c, north_c[rows - 1:]), north_c)
    west_c = ocean * jnp.where(col_ids == 0, upright(coef_cols_in[:1]), west_raw)
    south_c = ocean * jnp.where(row_ids == 0, coef_rows[1][7:8], south_raw)
    east_c, north_c = ocean * east_c, ocean * north_c
    centre = diag[...] + ((east_c + west_c) + (north_c + south_c))
    last_panel = slice(cols - 128, cols)
    east_edge = jnp.where(col_ids == cols - 1, east_c, 0.0)[:, last_panel]
    west_edge = jnp.where(col_ids == 0, west_c, 0.0)[:, :128]
    north_edge, south_edge = north_c[rows - 1:], south_c[:1]
    inside = (jnp.where(col_ids == cols - 1, 0.0, east_c),
              jnp.where(col_ids == 0, 0.0, west_c),
              jnp.where(row_ids == rows - 1, 0.0, north_c),
              jnp.where(row_ids == 0, 0.0, south_c))
    base_row = jnp.where(row_ids == 0, 1.0, 0.0)[:8]
    top_row = jnp.where(row_ids == rows - 1, 1.0, 0.0)[rows - 8:]

    def interior(k, field):
        terms = [coef * other for coef, other in zip(inside, rolled(held[k]))]
        return centre * field - ((terms[0] + terms[1]) + (terms[2] + terms[3]))

    def with_edges(k, image):
        block = rows_in[k, NORTH]
        above = jnp.where(is_top, mirrored(block), block[:1])
        below = rows_in[k, SOUTH][7:8]
        image = jnp.concatenate([
            image[:8] - base_row * (south_edge * below),
            image[8:rows - 8],
            image[rows - 8:] - top_row * (north_edge * above)], axis=0)
        return jnp.concatenate([
            image[:, :128] - west_edge * upright(cols_in[k, 0][:1]),
            *([image[:, 128:cols - 128]] if cols > 256 else []),
            image[:, last_panel] - east_edge * upright(cols_in[k, 1][:1])], axis=1)

    image = with_edges(0, interior(0, v0))
    held[1] = ocean * image
    send_halo(1)
    await_all(row_in, guess_recv.at[0])
    guessed = guessed + jnp.sum(row_in[...], axis=0)
    guess_out[1] = guessed
    lax.fori_loop(1, lats, start_column, 0)
    plain = interior(1, image)
    take_halo(1)
    second = with_edges(1, plain)
    await_all(column_in, guess_recv.at[1])
    packed = guessed + jnp.sum(column_in[...], axis=0)
    norm = pick(packed, 0)
    shift = pick(packed, 1) / norm
    spread = pick(packed, 2) / norm - shift * shift
    sigma = jnp.sqrt(jnp.maximum(spread, 1e-4 * shift * shift))
    scale = 1.0 / sigma
    v1 = (image - shift * v0) * scale
    v2 = ((second - shift * image) * scale - shift * v1) * scale - v0
    held[2] = ocean * v2
    send_halo(2)
    v0_ref[...] = v0
    v1_ref[...] = v1
    v2_ref[...] = v2
    early = [dot(v0, v0), dot(v0, v1)]
    base3 = (interior(2, v2) - shift * v2) * scale - v1
    early += [dot(v0, v2), dot(v2, v2)]
    take_halo(2)
    v3 = base3 + with_edges(2, jnp.zeros_like(v0)) * scale
    held[3] = ocean * v3
    send_halo(3)
    v3_ref[...] = v3
    base4 = (interior(3, v3) - shift * v3) * scale - v2
    early += [dot(v0, v3), dot(v2, v3), dot(v3, v3)]
    early = pack(early)
    pl.semaphore_wait(all_in, lons - 1)
    take_halo(3)
    v4 = base4 + with_edges(3, jnp.zeros_like(v0)) * scale
    packed = jnp.where(lane == 7, dot(v3, v4), early)
    part_out[...] = packed
    share()
    v4_ref[...] = v4
    await_all(part_in, part_recv.at[0])
    packed = packed + jnp.sum(part_in[...], axis=0)

    p00, p01, p02, p22, p03, p23, p33, p34 = [pick(packed, k) for k in range(8)]
    moment = [p00, p01, p02, p03, p22 - p00 - p02, p23 - p01 - p03]
    moment.append(p33 - p00 - p02 - moment[4])
    moment.append(p34 - p01 - p03 - moment[5])
    gram = {}
    for i in range(ITERS + 1):
        for j in range(i, ITERS + 1):
            if i + j < 2 * ITERS:
                gram[i, j] = gram[j, i] = sum(moment[k] for k in range(j - i, i + j + 1, 2))

    def inner(a, b):
        total = None
        for i, x in enumerate(a):
            line = None
            for j, y in enumerate(b):
                term = gram[i, j] * y
                line = term if line is None else line + term
            total = x * line if total is None else total + x * line
        return total

    def image_of(a):
        out = []
        for k in range(len(a) + 1):
            term = shift * a[k] if k < len(a) else None
            for near in (k - 1, k + 1):
                if 0 <= near < len(a):
                    term = sigma * a[near] if term is None else term + sigma * a[near]
            out.append(term)
        return out

    one = jnp.ones((1, 1), f32)
    left, way, found = [one], [one], []
    rr = inner(left, left)
    for step in range(ITERS):
        along = image_of(way)
        alpha = rr / inner(way, along)
        found = [(found[k] + alpha * w) if k < len(found) else alpha * w for k, w in enumerate(way)]
        left = [(left[k] - alpha * a) if k < len(left) else -alpha * a for k, a in enumerate(along)]
        if step + 1 < ITERS:
            new = inner(left, left)
            ratio = new / rr
            way = [(left[k] + ratio * way[k]) if k < len(way) else left[k] for k in range(len(left))]
            rr = new

    weights = jnp.zeros((8, 128), f32)
    spot = 128 * lax.broadcasted_iota(jnp.int32, (8, 128), 0) + lax.broadcasted_iota(
        jnp.int32, (8, 128), 1)
    for k, weight in enumerate(found):
        weights = jnp.where(spot == k, weight, weights)
    for k, weight in enumerate(left):
        weights = jnp.where(spot == 128 + k, weight, weights)
    mix_ref[...] = weights

    for k in range(ITERS):
        end_halo(k)
    coef_east.wait_send()
    coef_fold.wait_send()
    await_all(row_in, guess_send.at[0])
    await_all(column_in, guess_send.at[1])
    await_all(part_in, part_send.at[0])


def combine(v0_ref, v1_ref, v2_ref, v3_ref, v4_ref, mix_ref, sol_ref, res_ref):
    basis = [ref[...] for ref in (v0_ref, v1_ref, v2_ref, v3_ref, v4_ref)]
    for line, size, out_ref in ((0, ITERS, sol_ref), (1, ITERS + 1, res_ref)):
        total = mix_ref[line:line + 1, 0:1] * basis[0]
        for k in range(1, size):
            total = total + mix_ref[line:line + 1, k:k + 1] * basis[k]
        out_ref[...] = total


def solution(mesh):
    lats, lons = mesh.shape["lat"], mesh.shape["lon"]
    count = lats * lons

    def local(right_side, diagonal, east_coef, north_coef, land_sea, fold_partner):
        rows, cols = right_side.shape
        block = lambda dtype=f32: pltpu.VMEM((rows, cols), dtype)
        dma = pltpu.SemaphoreType.DMA
        *basis, weights = pl.pallas_call(
            lambda *refs: kernel(lats, lons, *refs),
            out_shape=(pltpu.VMEM((rows, cols), f32),) * (ITERS + 1) + (pltpu.VMEM((8, 128), f32),),
            in_specs=[pl.BlockSpec(memory_space=pl.ANY)] * 6,
            out_specs=(pl.BlockSpec(memory_space=pltpu.VMEM),) * (ITERS + 2),
            scratch_shapes=[
                block(), block(), block(), block(), block(jnp.int32),
                pltpu.VMEM((1, cols), jnp.int32), dma((6,)),
                pltpu.VMEM((ITERS, rows, cols), f32),
                pltpu.VMEM((ITERS, 2, 8, rows), f32),
                pltpu.VMEM((ITERS, 2, 8, cols), f32),
                pltpu.VMEM((ITERS, 2, 8, rows), f32),
                pltpu.VMEM((8, rows), f32),
                pltpu.VMEM((2, 8, cols), f32),
                pltpu.VMEM((8, rows), f32),
                dma((ITERS, 4)), dma((ITERS, 4)), dma((2,)), dma((3,)),
                pltpu.VMEM((1, 128), f32),
                pltpu.VMEM((count - 1, 1, 128), f32),
                dma((1,)), dma((1,)), pltpu.SemaphoreType.REGULAR,
                pltpu.VMEM((2, 1, 128), f32),
                pltpu.VMEM((lons - 1, 1, 128), f32),
                pltpu.VMEM((lats - 1, 1, 128), f32),
                dma((2,)), dma((2,)),
            ],
            compiler_params=pltpu.CompilerParams(collective_id=0, has_side_effects=True),
            name="cg",
        )(right_side, diagonal, east_coef, north_coef, land_sea, fold_partner.reshape(1, cols))

        return pl.pallas_call(
            combine,
            out_shape=(jax.ShapeDtypeStruct((rows, cols), f32),) * 2,
            in_specs=[pl.BlockSpec(memory_space=pltpu.VMEM)] * (ITERS + 2),
            out_specs=(pl.BlockSpec(memory_space=pltpu.VMEM),) * 2,
            name="combine",
        )(*[pltpu.with_memory_space_constraint(x, pltpu.VMEM) for x in (*basis, weights)])

    placed = (P("lat", "lon"),) * 5 + (P("lon"),)
    return jax.shard_map(
        local, mesh=mesh, in_specs=placed,
        out_specs=(P("lat", "lon"), P("lat", "lon")), check_vma=False)
```

```python
import jax
import jax.numpy as jnp
from jax import lax
from jax.experimental import pallas as pl
from jax.experimental.pallas import tpu as pltpu
from jax.sharding import PartitionSpec as P

ITERS = 4
MESH = pl.DeviceIdType.MESH
NORTH, SOUTH, EAST, WEST = range(4)
f32 = jnp.float32


def kernel(lats, lons, rhs_hbm, diag_hbm, east_hbm, north_hbm, land_hbm, partner_hbm,
           v0_ref, v1_ref, v2_ref, v3_ref, v4_ref, mix_ref,
           rhs, diag, east, north, land, partner, load_sem,
           held, cols_out, rows_in, cols_in, coef_cols, coef_rows, coef_cols_in,
           send_sem, recv_sem, coef_send, coef_recv,
           part_out, part_in, part_send, part_recv, all_in,
           guess_out, row_in, column_in, guess_send, guess_recv):
    rows, cols = rhs.shape
    lat, lon = lax.axis_index("lat"), lax.axis_index("lon")
    on_top, on_bottom = lat == lats - 1, lat == 0

    loads = [
        pltpu.make_async_copy(src, dst, load_sem.at[i])
        for i, (src, dst) in enumerate(
            ((rhs_hbm, rhs), (land_hbm, land), (east_hbm, east), (north_hbm, north),
             (partner_hbm, partner), (diag_hbm, diag)))
    ]
    for load in loads:
        load.start()

    barrier = pltpu.get_barrier_semaphore()

    def greet_lat(step, carry):
        pl.semaphore_signal(barrier, inc=1, device_id=(lax.rem(lat + step, lats), lon), device_id_type=MESH)
        return carry

    def greet_lon(step, carry):
        pl.semaphore_signal(barrier, inc=1, device_id=(lat, lax.rem(lon + step, lons)), device_id_type=MESH)
        return carry

    def pass_on(step, carry):
        pl.semaphore_signal(all_in, inc=1, device_id=(lat, lax.rem(lon + step, lons)), device_id_type=MESH)
        return carry

    lax.fori_loop(1, lons, greet_lon, 0)
    lax.fori_loop(1, lats, greet_lat, 0)

    east_id = (lat, lax.rem(lon + 1, lons))
    west_id = (lat, lax.rem(lon + lons - 1, lons))
    north_id = (lax.rem(lat + 1, lats), lon)
    south_id = (lax.rem(lat + lats - 1, lats), lon)
    fold_id = (lat, lons - 1 - lon)

    row_ids = lax.broadcasted_iota(jnp.int32, (rows, cols), 0)
    col_ids = lax.broadcasted_iota(jnp.int32, (rows, cols), 1)
    eye = lax.broadcasted_iota(jnp.int32, (rows, rows), 0) == lax.broadcasted_iota(
        jnp.int32, (rows, rows), 1)
    lane = lax.broadcasted_iota(jnp.int32, (1, 128), 1)

    def flat(column):
        return jnp.sum(jnp.where(eye, column, 0.0), axis=0, keepdims=True)

    def upright(row):
        return jnp.sum(jnp.where(eye, row, 0.0), axis=1, keepdims=True)

    for load in loads[:-1]:
        load.wait()
    ocean = land[...].astype(f32)
    east_c = east[...]
    coef_cols[...] = jnp.broadcast_to(flat(east_c[:, cols - 1:]), (8, rows))
    v0 = rhs[...]
    masked = ocean * v0
    held[0] = masked
    north_c = north[...]

    def rolled(field):
        return (pltpu.roll(field, cols - 1, 1), pltpu.roll(field, 1, 1),
                pltpu.roll(field, rows - 1, 0), pltpu.roll(field, 1, 0))

    def dot(a, b):
        return jnp.sum(jnp.sum(a * b, axis=0, keepdims=True), axis=1, keepdims=True)

    def pick(packed, k):
        return packed[:, k:k + 1]

    def pack(values):
        packed = jnp.zeros((1, 128), f32)
        for k, value in enumerate(values):
            packed = jnp.where(lane == k, value, packed)
        return packed

    west_raw, south_raw = pltpu.roll(east_c, 1, 1), pltpu.roll(north_c, 1, 0)
    own = lax.rem(partner[...], cols)
    lower = jnp.broadcast_to(lax.rem(own, 128), (8, cols))
    panel = jnp.broadcast_to(own // 128, (8, cols))

    def mirrored(block):
        pieces = []
        for at in range(0, cols, 128):
            index = lower[:, at:at + 128]
            which = panel[:, at:at + 128]
            picked = jnp.zeros((8, 128), f32)
            for k in range(cols // 128):
                found = jnp.take_along_axis(block[:, k * 128:(k + 1) * 128], index, axis=1)
                picked = jnp.where(which == k, found, picked)
            pieces.append(picked)
        return jnp.concatenate(pieces, axis=1)[7:8]

    @pl.when(on_bottom)
    def _():
        for k in range(ITERS):
            rows_in[k, SOUTH] = jnp.zeros((8, cols), f32)
        coef_rows[1] = jnp.zeros((8, cols), f32)

    def strip_columns(k, field):
        cols_out[k, 0] = jnp.broadcast_to(flat(field[:, cols - 1:]), (8, rows))
        cols_out[k, 1] = jnp.broadcast_to(flat(field[:, :1]), (8, rows))

    strip_columns(0, masked)
    pl.semaphore_wait(barrier, lats + lons - 2)

    def remote(src, dst, send, recv, to):
        return pltpu.make_async_remote_copy(
            src_ref=src, dst_ref=dst, send_sem=send, recv_sem=recv,
            device_id=to, device_id_type=MESH)

    def halo_copies(k):
        top, base = held.at[k, pl.ds(rows - 8, 8)], held.at[k, pl.ds(0, 8)]
        sems = lambda way: (send_sem.at[k, way], recv_sem.at[k, way])
        to_east = remote(cols_out.at[k, 0], cols_in.at[k, 0], *sems(WEST), east_id)
        to_west = remote(cols_out.at[k, 1], cols_in.at[k, 1], *sems(EAST), west_id)
        to_fold = remote(top, rows_in.at[k, NORTH], *sems(NORTH), fold_id)
        to_north = remote(top, rows_in.at[k, SOUTH], send_sem.at[k, NORTH], recv_sem.at[k, SOUTH], north_id)
        to_south = remote(base, rows_in.at[k, NORTH], send_sem.at[k, SOUTH], recv_sem.at[k, NORTH], south_id)
        return to_east, to_west, to_fold, to_north, to_south

    coef_east = remote(coef_cols, coef_cols_in, coef_send.at[0], coef_recv.at[0], east_id)
    coef_top = north.at[pl.ds(rows - 8, 8)]
    coef_fold = remote(coef_top, coef_rows.at[0], coef_send.at[1], coef_recv.at[1], fold_id)
    coef_north = remote(coef_top, coef_rows.at[1], coef_send.at[1], coef_recv.at[2], north_id)

    coef_east.start()

    @pl.when(on_top)
    def _():
        coef_fold.start()

    @pl.when(jnp.logical_not(on_top))
    def _():
        coef_north.start()

    def send_halo(k):
        to_east, to_west, to_fold, to_north, to_south = halo_copies(k)

        @pl.when(on_top)
        def _():
            to_fold.start()

        @pl.when(jnp.logical_not(on_top))
        def _():
            to_north.start()

        @pl.when(jnp.logical_not(on_bottom))
        def _():
            to_south.start()

        if k:
            strip_columns(k, held[k])
        to_east.start()
        to_west.start()

    def take_halo(k):
        to_east, to_west, to_fold, to_north, to_south = halo_copies(k)
        to_east.wait_recv()
        to_west.wait_recv()
        to_south.wait_recv()

        @pl.when(jnp.logical_not(on_bottom))
        def _():
            to_north.wait_recv()

    def end_halo(k):
        to_east, to_west, to_fold, to_north, to_south = halo_copies(k)
        to_east.wait_send()
        to_west.wait_send()
        to_north.wait_send()

        @pl.when(jnp.logical_not(on_bottom))
        def _():
            to_south.wait_send()

    def lon_at(step):
        return (lat, lax.rem(lon + step, lons))

    def lat_at(step):
        return (lax.rem(lat + step, lats), lon)

    def row_copy(step):
        return remote(guess_out.at[0], row_in.at[step - 1], guess_send.at[0], guess_recv.at[0], lon_at(step))

    def column_copy(step):
        return remote(guess_out.at[1], column_in.at[step - 1], guess_send.at[1], guess_recv.at[1], lat_at(step))

    def part_copy(up, right):
        to = (lax.rem(lat + up, lats), lax.rem(lon + right, lons))
        return remote(part_out, part_in.at[up * lons + right - 1], part_send.at[0], part_recv.at[0], to)

    def start_row(step, carry):
        row_copy(step).start()
        return carry

    def start_column(step, carry):
        column_copy(step).start()
        return carry

    def await_all(whole, sem):
        pltpu.make_async_copy(whole, whole, sem).wait()

    def share():
        for up in reversed(range(lats)):
            def send(right, carry):
                part_copy(up, right).start()
                return carry

            lax.fori_loop(0 if up else 1, lons, send, 0)

    send_halo(0)
    loads[-1].wait()
    guess = diag[...] * v0
    for coef, other in zip((east_c, west_raw, north_c, south_raw), rolled(masked)):
        guess = guess + ocean * (coef * (masked - other))
    guessed = pack((dot(v0, v0), dot(v0, guess), dot(guess, guess)))
    guess_out[0] = guessed
    lax.fori_loop(1, lons, start_row, 0)
    lax.fori_loop(1, lons, pass_on, 0)
    take_halo(0)
    coef_east.wait_recv()

    @pl.when(on_top)
    def _():
        coef_fold.wait_recv()

    @pl.when(jnp.logical_not(on_bottom))
    def _():
        coef_north.wait_recv()

    top_flag = jnp.where(on_top, 1, 0)
    is_top = jnp.full((1, cols), top_flag, jnp.int32) == 1
    coef_mirror = jnp.where(is_top, coef_rows[0], 0.0)
    fold_c = 0.5 * (north_c[rows - 1:] + mirrored(coef_mirror))
    north_c = jnp.where(
        row_ids == rows - 1, jnp.where(is_top, fold_c, north_c[rows - 1:]), north_c)
    west_c = ocean * jnp.where(col_ids == 0, upright(coef_cols_in[:1]), west_raw)
    south_c = ocean * jnp.where(row_ids == 0, coef_rows[1][7:8], south_raw)
    east_c, north_c = ocean * east_c, ocean * north_c
    centre = diag[...] + ((east_c + west_c) + (north_c + south_c))
    last_panel = slice(cols - 128, cols)
    east_edge = jnp.where(col_ids == cols - 1, east_c, 0.0)[:, last_panel]
    west_edge = jnp.where(col_ids == 0, west_c, 0.0)[:, :128]
    north_edge, south_edge = north_c[rows - 1:], south_c[:1]
    inside = (jnp.where(col_ids == cols - 1, 0.0, east_c),
              jnp.where(col_ids == 0, 0.0, west_c),
              jnp.where(row_ids == rows - 1, 0.0, north_c),
              jnp.where(row_ids == 0, 0.0, south_c))
    base_row = jnp.where(row_ids == 0, 1.0, 0.0)[:8]
    top_row = jnp.where(row_ids == rows - 1, 1.0, 0.0)[rows - 8:]

    def interior(k, field):
        terms = [coef * other for coef, other in zip(inside, rolled(held[k]))]
        return centre * field - ((terms[0] + terms[1]) + (terms[2] + terms[3]))

    def with_edges(k, image):
        block = rows_in[k, NORTH]
        above = jnp.where(is_top, mirrored(block), block[:1])
        below = rows_in[k, SOUTH][7:8]
        image = jnp.concatenate([
            image[:8] - base_row * (south_edge * below),
            image[8:rows - 8],
            image[rows - 8:] - top_row * (north_edge * above)], axis=0)
        return jnp.concatenate([
            image[:, :128] - west_edge * upright(cols_in[k, 0][:1]),
            *([image[:, 128:cols - 128]] if cols > 256 else []),
            image[:, last_panel] - east_edge * upright(cols_in[k, 1][:1])], axis=1)

    image = with_edges(0, interior(0, v0))
    held[1] = ocean * image
    send_halo(1)
    await_all(row_in, guess_recv.at[0])
    guessed = guessed + jnp.sum(row_in[...], axis=0)
    guess_out[1] = guessed
    lax.fori_loop(1, lats, start_column, 0)
    plain = interior(1, image)
    take_halo(1)
    second = with_edges(1, plain)
    await_all(column_in, guess_recv.at[1])
    packed = guessed + jnp.sum(column_in[...], axis=0)
    norm = pick(packed, 0)
    shift = pick(packed, 1) / norm
    spread = pick(packed, 2) / norm - shift * shift
    sigma = jnp.sqrt(jnp.maximum(spread, 1e-4 * shift * shift))
    scale = 1.0 / sigma
    v1 = (image - shift * v0) * scale
    v2 = ((second - shift * image) * scale - shift * v1) * scale - v0
    held[2] = ocean * v2
    send_halo(2)
    v0_ref[...] = v0
    v1_ref[...] = v1
    v2_ref[...] = v2
    early = [dot(v0, v0), dot(v0, v1)]
    base3 = (interior(2, v2) - shift * v2) * scale - v1
    early += [dot(v0, v2), dot(v2, v2)]
    take_halo(2)
    v3 = base3 + with_edges(2, jnp.zeros_like(v0)) * scale
    held[3] = ocean * v3
    send_halo(3)
    v3_ref[...] = v3
    base4 = (interior(3, v3) - shift * v3) * scale - v2
    early += [dot(v0, v3), dot(v2, v3), dot(v3, v3)]
    early = pack(early)
    pl.semaphore_wait(all_in, lons - 1)
    take_halo(3)
    v4 = base4 + with_edges(3, jnp.zeros_like(v0)) * scale
    packed = jnp.where(lane == 7, dot(v3, v4), early)
    part_out[...] = packed
    share()
    v4_ref[...] = v4
    await_all(part_in, part_recv.at[0])
    packed = packed + jnp.sum(part_in[...], axis=0)

    p00, p01, p02, p22, p03, p23, p33, p34 = [pick(packed, k) for k in range(8)]
    moment = [p00, p01, p02, p03, p22 - p00 - p02, p23 - p01 - p03]
    moment.append(p33 - p00 - p02 - moment[4])
    moment.append(p34 - p01 - p03 - moment[5])
    gram = {}
    for i in range(ITERS + 1):
        for j in range(i, ITERS + 1):
            if i + j < 2 * ITERS:
                gram[i, j] = gram[j, i] = sum(moment[k] for k in range(j - i, i + j + 1, 2))

    def inner(a, b):
        total = None
        for i, x in enumerate(a):
            line = None
            for j, y in enumerate(b):
                term = gram[i, j] * y
                line = term if line is None else line + term
            total = x * line if total is None else total + x * line
        return total

    def image_of(a):
        out = []
        for k in range(len(a) + 1):
            term = shift * a[k] if k < len(a) else None
            for near in (k - 1, k + 1):
                if 0 <= near < len(a):
                    term = sigma * a[near] if term is None else term + sigma * a[near]
            out.append(term)
        return out

    one = jnp.ones((1, 1), f32)
    left, way, found = [one], [one], []
    rr = inner(left, left)
    for step in range(ITERS):
        along = image_of(way)
        alpha = rr / inner(way, along)
        found = [(found[k] + alpha * w) if k < len(found) else alpha * w for k, w in enumerate(way)]
        left = [(left[k] - alpha * a) if k < len(left) else -alpha * a for k, a in enumerate(along)]
        if step + 1 < ITERS:
            new = inner(left, left)
            ratio = new / rr
            way = [(left[k] + ratio * way[k]) if k < len(way) else left[k] for k in range(len(left))]
            rr = new

    weights = jnp.zeros((8, 128), f32)
    spot = 128 * lax.broadcasted_iota(jnp.int32, (8, 128), 0) + lax.broadcasted_iota(
        jnp.int32, (8, 128), 1)
    for k, weight in enumerate(found):
        weights = jnp.where(spot == k, weight, weights)
    for k, weight in enumerate(left):
        weights = jnp.where(spot == 128 + k, weight, weights)
    mix_ref[...] = weights

    for k in range(ITERS):
        end_halo(k)
    coef_east.wait_send()
    coef_fold.wait_send()
    await_all(row_in, guess_send.at[0])
    await_all(column_in, guess_send.at[1])
    await_all(part_in, part_send.at[0])


def combine(v0_ref, v1_ref, v2_ref, v3_ref, v4_ref, mix_ref, sol_ref, res_ref):
    basis = [ref[...] for ref in (v0_ref, v1_ref, v2_ref, v3_ref, v4_ref)]
    for line, size, out_ref in ((0, ITERS, sol_ref), (1, ITERS + 1, res_ref)):
        total = mix_ref[line:line + 1, 0:1] * basis[0]
        for k in range(1, size):
            total = total + mix_ref[line:line + 1, k:k + 1] * basis[k]
        out_ref[...] = total


def solution(mesh):
    lats, lons = mesh.shape["lat"], mesh.shape["lon"]
    count = lats * lons

    def local(right_side, diagonal, east_coef, north_coef, land_sea, fold_partner):
        rows, cols = right_side.shape
        block = lambda dtype=f32: pltpu.VMEM((rows, cols), dtype)
        dma = pltpu.SemaphoreType.DMA
        *basis, weights = pl.pallas_call(
            lambda *refs: kernel(lats, lons, *refs),
            out_shape=(pltpu.VMEM((rows, cols), f32),) * (ITERS + 1) + (pltpu.VMEM((8, 128), f32),),
            in_specs=[pl.BlockSpec(memory_space=pl.ANY)] * 6,
            out_specs=(pl.BlockSpec(memory_space=pltpu.VMEM),) * (ITERS + 2),
            scratch_shapes=[
                block(), block(), block(), block(), block(jnp.int32),
                pltpu.VMEM((1, cols), jnp.int32), dma((6,)),
                pltpu.VMEM((ITERS, rows, cols), f32),
                pltpu.VMEM((ITERS, 2, 8, rows), f32),
                pltpu.VMEM((ITERS, 2, 8, cols), f32),
                pltpu.VMEM((ITERS, 2, 8, rows), f32),
                pltpu.VMEM((8, rows), f32),
                pltpu.VMEM((2, 8, cols), f32),
                pltpu.VMEM((8, rows), f32),
                dma((ITERS, 4)), dma((ITERS, 4)), dma((2,)), dma((3,)),
                pltpu.VMEM((1, 128), f32),
                pltpu.VMEM((count - 1, 1, 128), f32),
                dma((1,)), dma((1,)), pltpu.SemaphoreType.REGULAR,
                pltpu.VMEM((2, 1, 128), f32),
                pltpu.VMEM((lons - 1, 1, 128), f32),
                pltpu.VMEM((lats - 1, 1, 128), f32),
                dma((2,)), dma((2,)),
            ],
            compiler_params=pltpu.CompilerParams(collective_id=0, has_side_effects=True),
            name="cg",
        )(right_side, diagonal, east_coef, north_coef, land_sea, fold_partner.reshape(1, cols))

        return pl.pallas_call(
            combine,
            out_shape=(jax.ShapeDtypeStruct((rows, cols), f32),) * 2,
            in_specs=[pl.BlockSpec(memory_space=pltpu.VMEM)] * (ITERS + 2),
            out_specs=(pl.BlockSpec(memory_space=pltpu.VMEM),) * 2,
            name="combine",
        )(*[pltpu.with_memory_space_constraint(x, pltpu.VMEM) for x in (*basis, weights)])

    placed = (P("lat", "lon"),) * 5 + (P("lon"),)
    return jax.shard_map(
        local, mesh=mesh, in_specs=placed,
        out_specs=(P("lat", "lon"), P("lat", "lon")), check_vma=False)
```

```python
import jax
import jax.numpy as jnp
from jax import lax
from jax.experimental import pallas as pl
from jax.experimental.pallas import tpu as pltpu
from jax.sharding import PartitionSpec as P

ITERS = 4
MESH = pl.DeviceIdType.MESH
NORTH, SOUTH, EAST, WEST = range(4)
f32 = jnp.float32


def kernel(lats, lons, rhs_hbm, diag_hbm, east_hbm, north_hbm, land_hbm, partner_hbm,
           v0_ref, v1_ref, v2_ref, v3_ref, v4_ref, mix_ref,
           rhs, diag, east, north, land, partner, load_sem,
           held, cols_out, rows_in, cols_in, coef_cols, coef_rows, coef_cols_in,
           send_sem, recv_sem, coef_send, coef_recv,
           part_out, part_in, part_send, part_recv, all_in,
           guess_out, row_in, column_in, guess_send, guess_recv):
    rows, cols = rhs.shape
    lat, lon = lax.axis_index("lat"), lax.axis_index("lon")
    on_top, on_bottom = lat == lats - 1, lat == 0

    loads = [
        pltpu.make_async_copy(src, dst, load_sem.at[i])
        for i, (src, dst) in enumerate(
            ((rhs_hbm, rhs), (land_hbm, land), (east_hbm, east), (north_hbm, north),
             (partner_hbm, partner), (diag_hbm, diag)))
    ]
    for load in loads:
        load.start()

    barrier = pltpu.get_barrier_semaphore()

    def greet_lat(step, carry):
        pl.semaphore_signal(barrier, inc=1, device_id=(lax.rem(lat + step, lats), lon), device_id_type=MESH)
        return carry

    def greet_lon(step, carry):
        pl.semaphore_signal(barrier, inc=1, device_id=(lat, lax.rem(lon + step, lons)), device_id_type=MESH)
        return carry

    def pass_on(step, carry):
        pl.semaphore_signal(all_in, inc=1, device_id=(lat, lax.rem(lon + step, lons)), device_id_type=MESH)
        return carry

    lax.fori_loop(1, lons, greet_lon, 0)
    lax.fori_loop(1, lats, greet_lat, 0)

    east_id = (lat, lax.rem(lon + 1, lons))
    west_id = (lat, lax.rem(lon + lons - 1, lons))
    north_id = (lax.rem(lat + 1, lats), lon)
    south_id = (lax.rem(lat + lats - 1, lats), lon)
    fold_id = (lat, lons - 1 - lon)

    row_ids = lax.broadcasted_iota(jnp.int32, (rows, cols), 0)
    col_ids = lax.broadcasted_iota(jnp.int32, (rows, cols), 1)
    eye = lax.broadcasted_iota(jnp.int32, (rows, rows), 0) == lax.broadcasted_iota(
        jnp.int32, (rows, rows), 1)
    lane = lax.broadcasted_iota(jnp.int32, (1, 128), 1)

    def flat(column):
        return jnp.sum(jnp.where(eye, column, 0.0), axis=0, keepdims=True)

    def upright(row):
        return jnp.sum(jnp.where(eye, row, 0.0), axis=1, keepdims=True)

    for load in loads[:-1]:
        load.wait()
    ocean = land[...].astype(f32)
    east_c = east[...]
    coef_cols[...] = jnp.broadcast_to(flat(east_c[:, cols - 1:]), (8, rows))
    v0 = rhs[...]
    masked = ocean * v0
    held[0] = masked
    north_c = north[...]

    def rolled(field):
        return (pltpu.roll(field, cols - 1, 1), pltpu.roll(field, 1, 1),
                pltpu.roll(field, rows - 1, 0), pltpu.roll(field, 1, 0))

    def dot(a, b):
        return jnp.sum(jnp.sum(a * b, axis=0, keepdims=True), axis=1, keepdims=True)

    def pick(packed, k):
        return packed[:, k:k + 1]

    def pack(values):
        packed = jnp.zeros((1, 128), f32)
        for k, value in enumerate(values):
            packed = jnp.where(lane == k, value, packed)
        return packed

    west_raw, south_raw = pltpu.roll(east_c, 1, 1), pltpu.roll(north_c, 1, 0)
    own = lax.rem(partner[...], cols)
    lower = jnp.broadcast_to(lax.rem(own, 128), (8, cols))
    panel = jnp.broadcast_to(own // 128, (8, cols))

    def mirrored(block):
        pieces = []
        for at in range(0, cols, 128):
            index = lower[:, at:at + 128]
            which = panel[:, at:at + 128]
            picked = jnp.zeros((8, 128), f32)
            for k in range(cols // 128):
                found = jnp.take_along_axis(block[:, k * 128:(k + 1) * 128], index, axis=1)
                picked = jnp.where(which == k, found, picked)
            pieces.append(picked)
        return jnp.concatenate(pieces, axis=1)[7:8]

    @pl.when(on_bottom)
    def _():
        for k in range(ITERS):
            rows_in[k, SOUTH] = jnp.zeros((8, cols), f32)
        coef_rows[1] = jnp.zeros((8, cols), f32)

    def strip_columns(k, field):
        cols_out[k, 0] = jnp.broadcast_to(flat(field[:, cols - 1:]), (8, rows))
        cols_out[k, 1] = jnp.broadcast_to(flat(field[:, :1]), (8, rows))

    strip_columns(0, masked)
    pl.semaphore_wait(barrier, lats + lons - 2)

    def remote(src, dst, send, recv, to):
        return pltpu.make_async_remote_copy(
            src_ref=src, dst_ref=dst, send_sem=send, recv_sem=recv,
            device_id=to, device_id_type=MESH)

    def halo_copies(k):
        top, base = held.at[k, pl.ds(rows - 8, 8)], held.at[k, pl.ds(0, 8)]
        sems = lambda way: (send_sem.at[k, way], recv_sem.at[k, way])
        to_east = remote(cols_out.at[k, 0], cols_in.at[k, 0], *sems(WEST), east_id)
        to_west = remote(cols_out.at[k, 1], cols_in.at[k, 1], *sems(EAST), west_id)
        to_fold = remote(top, rows_in.at[k, NORTH], *sems(NORTH), fold_id)
        to_north = remote(top, rows_in.at[k, SOUTH], send_sem.at[k, NORTH], recv_sem.at[k, SOUTH], north_id)
        to_south = remote(base, rows_in.at[k, NORTH], send_sem.at[k, SOUTH], recv_sem.at[k, NORTH], south_id)
        return to_east, to_west, to_fold, to_north, to_south

    coef_east = remote(coef_cols, coef_cols_in, coef_send.at[0], coef_recv.at[0], east_id)
    coef_top = north.at[pl.ds(rows - 8, 8)]
    coef_fold = remote(coef_top, coef_rows.at[0], coef_send.at[1], coef_recv.at[1], fold_id)
    coef_north = remote(coef_top, coef_rows.at[1], coef_send.at[1], coef_recv.at[2], north_id)

    coef_east.start()

    @pl.when(on_top)
    def _():
        coef_fold.start()

    @pl.when(jnp.logical_not(on_top))
    def _():
        coef_north.start()

    def send_halo(k):
        to_east, to_west, to_fold, to_north, to_south = halo_copies(k)

        @pl.when(on_top)
        def _():
            to_fold.start()

        @pl.when(jnp.logical_not(on_top))
        def _():
            to_north.start()

        @pl.when(jnp.logical_not(on_bottom))
        def _():
            to_south.start()

        if k:
            strip_columns(k, held[k])
        to_east.start()
        to_west.start()

    def take_halo(k):
        to_east, to_west, to_fold, to_north, to_south = halo_copies(k)
        to_east.wait_recv()
        to_west.wait_recv()
        to_south.wait_recv()

        @pl.when(jnp.logical_not(on_bottom))
        def _():
            to_north.wait_recv()

    def end_halo(k):
        to_east, to_west, to_fold, to_north, to_south = halo_copies(k)
        to_east.wait_send()
        to_west.wait_send()
        to_north.wait_send()

        @pl.when(jnp.logical_not(on_bottom))
        def _():
            to_south.wait_send()

    def lon_at(step):
        return (lat, lax.rem(lon + step, lons))

    def lat_at(step):
        return (lax.rem(lat + step, lats), lon)

    def row_copy(step):
        return remote(guess_out.at[0], row_in.at[step - 1], guess_send.at[0], guess_recv.at[0], lon_at(step))

    def column_copy(step):
        return remote(guess_out.at[1], column_in.at[step - 1], guess_send.at[1], guess_recv.at[1], lat_at(step))

    def part_copy(up, right):
        to = (lax.rem(lat + up, lats), lax.rem(lon + right, lons))
        return remote(part_out, part_in.at[up * lons + right - 1], part_send.at[0], part_recv.at[0], to)

    def start_row(step, carry):
        row_copy(step).start()
        return carry

    def start_column(step, carry):
        column_copy(step).start()
        return carry

    def await_all(whole, sem):
        pltpu.make_async_copy(whole, whole, sem).wait()

    def share():
        for up in reversed(range(lats)):
            def send(right, carry):
                part_copy(up, right).start()
                return carry

            lax.fori_loop(0 if up else 1, lons, send, 0)

    send_halo(0)
    loads[-1].wait()
    guess = diag[...] * v0
    for coef, other in zip((east_c, west_raw, north_c, south_raw), rolled(masked)):
        guess = guess + ocean * (coef * (masked - other))
    guessed = pack((dot(v0, v0), dot(v0, guess), dot(guess, guess)))
    guess_out[0] = guessed
    lax.fori_loop(1, lons, start_row, 0)
    lax.fori_loop(1, lons, pass_on, 0)
    take_halo(0)
    coef_east.wait_recv()

    @pl.when(on_top)
    def _():
        coef_fold.wait_recv()

    @pl.when(jnp.logical_not(on_bottom))
    def _():
        coef_north.wait_recv()

    top_flag = jnp.where(on_top, 1, 0)
    is_top = jnp.full((1, cols), top_flag, jnp.int32) == 1
    coef_mirror = jnp.where(is_top, coef_rows[0], 0.0)
    fold_c = 0.5 * (north_c[rows - 1:] + mirrored(coef_mirror))
    north_c = jnp.where(
        row_ids == rows - 1, jnp.where(is_top, fold_c, north_c[rows - 1:]), north_c)
    west_c = ocean * jnp.where(col_ids == 0, upright(coef_cols_in[:1]), west_raw)
    south_c = ocean * jnp.where(row_ids == 0, coef_rows[1][7:8], south_raw)
    east_c, north_c = ocean * east_c, ocean * north_c
    centre = diag[...] + ((east_c + west_c) + (north_c + south_c))
    last_panel = slice(cols - 128, cols)
    east_edge = jnp.where(col_ids == cols - 1, east_c, 0.0)[:, last_panel]
    west_edge = jnp.where(col_ids == 0, west_c, 0.0)[:, :128]
    north_edge, south_edge = north_c[rows - 1:], south_c[:1]
    inside = (jnp.where(col_ids == cols - 1, 0.0, east_c),
              jnp.where(col_ids == 0, 0.0, west_c),
              jnp.where(row_ids == rows - 1, 0.0, north_c),
              jnp.where(row_ids == 0, 0.0, south_c))
    base_row = jnp.where(row_ids == 0, 1.0, 0.0)[:8]
    top_row = jnp.where(row_ids == rows - 1, 1.0, 0.0)[rows - 8:]

    def interior(k, field):
        terms = [coef * other for coef, other in zip(inside, rolled(held[k]))]
        return centre * field - ((terms[0] + terms[1]) + (terms[2] + terms[3]))

    def with_edges(k, image):
        block = rows_in[k, NORTH]
        above = jnp.where(is_top, mirrored(block), block[:1])
        below = rows_in[k, SOUTH][7:8]
        image = jnp.concatenate([
            image[:8] - base_row * (south_edge * below),
            image[8:rows - 8],
            image[rows - 8:] - top_row * (north_edge * above)], axis=0)
        return jnp.concatenate([
            image[:, :128] - west_edge * upright(cols_in[k, 0][:1]),
            *([image[:, 128:cols - 128]] if cols > 256 else []),
            image[:, last_panel] - east_edge * upright(cols_in[k, 1][:1])], axis=1)

    image = with_edges(0, interior(0, v0))
    held[1] = ocean * image
    send_halo(1)
    await_all(row_in, guess_recv.at[0])
    guessed = guessed + jnp.sum(row_in[...], axis=0)
    guess_out[1] = guessed
    lax.fori_loop(1, lats, start_column, 0)
    plain = interior(1, image)
    take_halo(1)
    second = with_edges(1, plain)
    await_all(column_in, guess_recv.at[1])
    packed = guessed + jnp.sum(column_in[...], axis=0)
    norm = pick(packed, 0)
    shift = pick(packed, 1) / norm
    spread = pick(packed, 2) / norm - shift * shift
    sigma = jnp.sqrt(jnp.maximum(spread, 1e-4 * shift * shift))
    scale = 1.0 / sigma
    v1 = (image - shift * v0) * scale
    v2 = ((second - shift * image) * scale - shift * v1) * scale - v0
    held[2] = ocean * v2
    send_halo(2)
    v0_ref[...] = v0
    v1_ref[...] = v1
    v2_ref[...] = v2
    early = [dot(v0, v0), dot(v0, v1)]
    base3 = (interior(2, v2) - shift * v2) * scale - v1
    early += [dot(v0, v2), dot(v2, v2)]
    take_halo(2)
    v3 = base3 + with_edges(2, jnp.zeros_like(v0)) * scale
    held[3] = ocean * v3
    send_halo(3)
    v3_ref[...] = v3
    base4 = (interior(3, v3) - shift * v3) * scale - v2
    early += [dot(v0, v3), dot(v2, v3), dot(v3, v3)]
    early = pack(early)
    pl.semaphore_wait(all_in, lons - 1)
    take_halo(3)
    v4 = base4 + with_edges(3, jnp.zeros_like(v0)) * scale
    packed = jnp.where(lane == 7, dot(v3, v4), early)
    part_out[...] = packed
    share()
    v4_ref[...] = v4
    await_all(part_in, part_recv.at[0])
    packed = packed + jnp.sum(part_in[...], axis=0)

    p00, p01, p02, p22, p03, p23, p33, p34 = [pick(packed, k) for k in range(8)]
    moment = [p00, p01, p02, p03, p22 - p00 - p02, p23 - p01 - p03]
    moment.append(p33 - p00 - p02 - moment[4])
    moment.append(p34 - p01 - p03 - moment[5])
    gram = {}
    for i in range(ITERS + 1):
        for j in range(i, ITERS + 1):
            if i + j < 2 * ITERS:
                gram[i, j] = gram[j, i] = sum(moment[k] for k in range(j - i, i + j + 1, 2))

    def energy(i, j):
        total = shift * gram[i, j] + sigma * gram[i, j + 1]
        return total + sigma * gram[i, j - 1] if j else total

    system = {(i, j): energy(i, j) for i in range(ITERS) for j in range(i, ITERS)}
    goal = [gram[0, i] for i in range(ITERS)]
    inverse = []
    for k in range(ITERS):
        inverse.append(1.0 / system[k, k])
        for i in range(k + 1, ITERS):
            factor = system[k, i] * inverse[k]
            goal[i] = goal[i] - factor * goal[k]
            for j in range(i, ITERS):
                system[i, j] = system[i, j] - factor * system[k, j]
    found = [None] * ITERS
    for k in reversed(range(ITERS)):
        value = goal[k]
        for j in range(k + 1, ITERS):
            value = value - system[k, j] * found[j]
        found[k] = value * inverse[k]
    left = []
    for k in range(ITERS + 1):
        value = jnp.full((1, 1), 0.0 if k else 1.0, f32)
        if k < ITERS:
            value = value - shift * found[k]
        for near in (k - 1, k + 1):
            if 0 <= near < ITERS:
                value = value - sigma * found[near]
        left.append(value)

    weights = jnp.zeros((8, 128), f32)
    spot = 128 * lax.broadcasted_iota(jnp.int32, (8, 128), 0) + lax.broadcasted_iota(
        jnp.int32, (8, 128), 1)
    for k, weight in enumerate(found):
        weights = jnp.where(spot == k, weight, weights)
    for k, weight in enumerate(left):
        weights = jnp.where(spot == 128 + k, weight, weights)
    mix_ref[...] = weights

    for k in range(ITERS):
        end_halo(k)
    coef_east.wait_send()
    coef_fold.wait_send()
    await_all(row_in, guess_send.at[0])
    await_all(column_in, guess_send.at[1])
    await_all(part_in, part_send.at[0])


def combine(v0_ref, v1_ref, v2_ref, v3_ref, v4_ref, mix_ref, sol_ref, res_ref):
    basis = [ref[...] for ref in (v0_ref, v1_ref, v2_ref, v3_ref, v4_ref)]
    for line, size, out_ref in ((0, ITERS, sol_ref), (1, ITERS + 1, res_ref)):
        total = mix_ref[line:line + 1, 0:1] * basis[0]
        for k in range(1, size):
            total = total + mix_ref[line:line + 1, k:k + 1] * basis[k]
        out_ref[...] = total


def solution(mesh):
    lats, lons = mesh.shape["lat"], mesh.shape["lon"]
    count = lats * lons

    def local(right_side, diagonal, east_coef, north_coef, land_sea, fold_partner):
        rows, cols = right_side.shape
        block = lambda dtype=f32: pltpu.VMEM((rows, cols), dtype)
        dma = pltpu.SemaphoreType.DMA
        *basis, weights = pl.pallas_call(
            lambda *refs: kernel(lats, lons, *refs),
            out_shape=(pltpu.VMEM((rows, cols), f32),) * (ITERS + 1) + (pltpu.VMEM((8, 128), f32),),
            in_specs=[pl.BlockSpec(memory_space=pl.ANY)] * 6,
            out_specs=(pl.BlockSpec(memory_space=pltpu.VMEM),) * (ITERS + 2),
            scratch_shapes=[
                block(), block(), block(), block(), block(jnp.int32),
                pltpu.VMEM((1, cols), jnp.int32), dma((6,)),
                pltpu.VMEM((ITERS, rows, cols), f32),
                pltpu.VMEM((ITERS, 2, 8, rows), f32),
                pltpu.VMEM((ITERS, 2, 8, cols), f32),
                pltpu.VMEM((ITERS, 2, 8, rows), f32),
                pltpu.VMEM((8, rows), f32),
                pltpu.VMEM((2, 8, cols), f32),
                pltpu.VMEM((8, rows), f32),
                dma((ITERS, 4)), dma((ITERS, 4)), dma((2,)), dma((3,)),
                pltpu.VMEM((1, 128), f32),
                pltpu.VMEM((count - 1, 1, 128), f32),
                dma((1,)), dma((1,)), pltpu.SemaphoreType.REGULAR,
                pltpu.VMEM((2, 1, 128), f32),
                pltpu.VMEM((lons - 1, 1, 128), f32),
                pltpu.VMEM((lats - 1, 1, 128), f32),
                dma((2,)), dma((2,)),
            ],
            compiler_params=pltpu.CompilerParams(collective_id=0, has_side_effects=True),
            name="cg",
        )(right_side, diagonal, east_coef, north_coef, land_sea, fold_partner.reshape(1, cols))

        return pl.pallas_call(
            combine,
            out_shape=(jax.ShapeDtypeStruct((rows, cols), f32),) * 2,
            in_specs=[pl.BlockSpec(memory_space=pltpu.VMEM)] * (ITERS + 2),
            out_specs=(pl.BlockSpec(memory_space=pltpu.VMEM),) * 2,
            name="combine",
        )(*[pltpu.with_memory_space_constraint(x, pltpu.VMEM) for x in (*basis, weights)])

    placed = (P("lat", "lon"),) * 5 + (P("lon"),)
    return jax.shard_map(
        local, mesh=mesh, in_specs=placed,
        out_specs=(P("lat", "lon"), P("lat", "lon")), check_vma=False)
```
